1024 devices in a mesh: dom: 128 (over y, z, core), sub: 8 (over x).
Axes of the slice: x: 8, y: 8, z: 8, core: 2. Of those that a mesh axis runs over, the one named last changes fastest.
Arguments:
- basis: float32 [2, 16, 1048576], P(None, None, ('dom', 'sub')), may hold values from -6 to 6
- compact: float32 [2, 32, 16], replicated, may hold values from -1 to 1
- weights: float32 [2, 2, 32], replicated, may hold values from -5 to 5
- fresh: float32 [2, 32], replicated, may hold values from -1 to 1
- shifts: float32 [2, 2], replicated, may hold values from -1 to 1
- k_tiles: float32 [8192, 3, 128, 128], P(('dom', 'sub'))
- pattern: int32 [8192, 2], P(('dom', 'sub')), may hold values from 0 to 63
- mass: float32 [1048576], P(('dom', 'sub')), may hold values from 0.5 to 2
- precond: float32 [8192, 2, 128, 128], P(('dom', 'sub'))
- c_tiles: float32 [8192, 128, 128], P(('dom', 'sub')), may hold values from -0.5 to 0.5
- c_rows: int32 [8192], P(('dom', 'sub')), may hold values from 0 to 7
- c_side: int32 [8192], P(('dom', 'sub')), may hold values from 0 to 1
- c_count: int32 [1024], P(('dom', 'sub')), may hold values from 1 to 8, as said below
Outputs:
- new_basis: float32 [2, 2, 1048576], P(None, None, ('dom', 'sub'))
- coeffs: float32 [2, 2, 18], replicated
The draws below stay inside these ranges and needn't reach their ends.
Inputs may be any that keep to these rules, and one draw needn't show every extreme that they name: `pattern`: each tile row's coupled tiles lie in its own domain group. `c_rows`: a tile row of the device itself. `c_side`: 0 reads the domain below, 1 the domain above. The live slots of device d are its first c_count[d]; some device has all 8 live.
All inputs are finite; a program needn't handle non-finite values.
Results may differ from the reference program's by a relative error of at most 0.0003.
Values sent between devices are 32-bit elements; how exact they have to be, the bound alone decides.
A program may use at most 32 MiB of HBM per device.

```python
import math
import jax
import jax.numpy as jnp
from jax import lax

TILE = 128
TD = 8
NOFF = 2
CMAX = 8
NT = 32
NB = 16
ITERS = 3
STEPS = 2
TILES = 8192
ROWS = 1048576
SLOTS = 8192
N_DOM = 128
N_SUB = 8
DEVICES = 1024


def draw_k_tiles(key, part):
    shape = (TILES, NOFF + 1, TILE, TILE)
    noise = jax.random.normal(key, shape, jnp.float32)
    noise = noise / jnp.sqrt(jnp.float32(TILE))
    return noise.at[:, 0].add(5.0 * jnp.eye(TILE, dtype=jnp.float32))


def draw_precond(key, part):
    shape = (TILES, 2, TILE, TILE)
    noise = jax.random.normal(key, shape, jnp.float32)
    noise = 0.08 * noise / jnp.sqrt(jnp.float32(TILE))
    return noise.at[:, 0].add(0.2 * jnp.eye(TILE, dtype=jnp.float32))


def draw_c_count(key, part):
    first, second, third = jax.random.split(jax.random.fold_in(key, 11), 3)
    light = jax.random.randint(first, (DEVICES,), 1, CMAX // 4 + 2)
    heavy = jax.random.randint(second, (DEVICES,), 0, 8) == 0
    counts = jnp.where(heavy, CMAX, light)
    spot = jax.random.randint(third, (), 0, DEVICES)
    return counts.at[spot].set(CMAX).astype(jnp.int32)


def place_ends(entries, key, least, largest):
    shape = entries.shape
    spot = [jax.random.randint(jax.random.fold_in(key, axis), (), 0, shape[axis]) for axis in range(len(shape))]
    entries = entries.at[tuple(spot)].set(least)
    longest = shape.index(max(shape))
    spot[longest] = (spot[longest] + 1) % shape[longest]
    return entries.at[tuple(spot)].set(largest)


def levels(rng, extent, pieces, low, largest):
    gain, own = 1.0, jax.random.fold_in(rng, 6)
    for position, parts in pieces:
        steps = jnp.exp(jax.random.uniform(jax.random.fold_in(own, position), (parts,), jnp.float32, low / len(pieces), largest / len(pieces)))
        gain = gain * jnp.repeat(steps, extent[position] // parts).reshape([-1 if axis == position else 1 for axis in range(len(extent))])
    return gain


def bell_draw(rng, extent, width, bound, shards=(), kind=jnp.bfloat16):
    loudness = levels(rng, extent, shards, -0.22, 0.18) if shards else 1.0
    entries = jax.random.normal(rng, extent, jnp.float32) * width * loudness
    return jnp.minimum(jnp.maximum(entries, -bound), bound).astype(kind)


def setup_inputs(seed: int = 0) -> dict:
    arg_keys = jax.random.split(jax.random.key(seed), 14)
    basis = bell_draw(arg_keys[0], (2, NB, ROWS), 1.0, 6.0, ((2, 1024),), jnp.float32)
    compact = bell_draw(arg_keys[1], (2, NT, NB), NT ** -0.5, 1.0, (), jnp.float32)
    weights = bell_draw(arg_keys[2], (STEPS, 2, NT), 1.0, 5.0, (), jnp.float32)
    fresh = bell_draw(arg_keys[3], (2, NT), NT ** -0.5, 1.0, (), jnp.float32)
    shifts = jnp.clip(jax.random.uniform(arg_keys[4], (STEPS, 2), jnp.float32, -1.0, 1.0), -1.0, 1.0)
    k_tiles = draw_k_tiles(jax.random.fold_in(arg_keys[13], 71), 0)
    pattern = place_ends(jax.random.randint(arg_keys[6], (TILES, NOFF), 0, TD * N_SUB), jax.random.fold_in(arg_keys[6], 1), 0, (TD * N_SUB) - 1).astype(jnp.int32)
    mass = jnp.clip(jnp.exp(math.log(2.0) - 1.3862944 * jax.random.uniform(arg_keys[7], (ROWS,), jnp.float32) ** levels(arg_keys[7], (ROWS,), ((0, 1024),), -0.2, 0.2)), 0.5, 2.0)
    precond = draw_precond(jax.random.fold_in(arg_keys[13], 71), 0)
    c_tiles = bell_draw(arg_keys[9], (SLOTS, TILE, TILE), TILE ** -0.5, 0.5, ((0, 1024),), jnp.float32)
    c_rows = place_ends(jax.random.randint(arg_keys[10], (SLOTS,), 0, TD), jax.random.fold_in(arg_keys[10], 1), 0, TD - 1).astype(jnp.int32)
    c_side = place_ends(jax.random.randint(arg_keys[11], (SLOTS,), 0, 2), jax.random.fold_in(arg_keys[11], 1), 0, 1).astype(jnp.int32)
    c_count = draw_c_count(jax.random.fold_in(arg_keys[13], 71), 0)
    return {"basis": basis, "compact": compact, "weights": weights, "fresh": fresh, "shifts": shifts, "k_tiles": k_tiles, "pattern": pattern, "mass": mass, "precond": precond, "c_tiles": c_tiles, "c_rows": c_rows, "c_side": c_side, "c_count": c_count}


HIGH = lax.Precision.HIGHEST
EPSILON = 1e-06

def solve_normal(matrix, vector):
    order = vector.shape[0]
    lower = [[None] * order for number in range(order)]
    for target in range(order):
        for source in range(target + 1):
            value = matrix[target, source]
            for middle in range(source):
                value = value - lower[target][middle] * lower[source][middle]
            if target == source:
                lower[target][target] = jnp.sqrt(value)
            else:
                lower[target][source] = value / lower[source][source]
    forward = []
    for target in range(order):
        value = vector[target]
        for middle in range(target):
            value = value - lower[target][middle] * forward[middle]
        forward.append(value / lower[target][target])
    result = [None] * order
    for target in reversed(range(order)):
        value = forward[target]
        for middle in range(target + 1, order):
            value = value - lower[middle][target] * result[middle]
        result[target] = value / lower[target][target]
    return jnp.stack(result)

def combine(coef_real, coef_imag, stack):
    real = jnp.dot(coef_real, stack[0], precision=HIGH) - jnp.dot(coef_imag, stack[1], precision=HIGH)
    imag = jnp.dot(coef_real, stack[1], precision=HIGH) + jnp.dot(coef_imag, stack[0], precision=HIGH)
    return jnp.stack([real, imag])

def conj_products(stack, vector):
    real = jnp.dot(stack[0], vector[0], precision=HIGH) + jnp.dot(stack[1], vector[1], precision=HIGH)
    imag = jnp.dot(stack[0], vector[1], precision=HIGH) - jnp.dot(stack[1], vector[0], precision=HIGH)
    return (real, imag)

def precondition(vector, precond):
    count, tile = (precond.shape[0], precond.shape[2])
    blocks = vector.reshape(2, count, tile)
    real = jnp.einsum('tij,tj->ti', precond[:, 0], blocks[0], precision=HIGH) - jnp.einsum('tij,tj->ti', precond[:, 1], blocks[1], precision=HIGH)
    imag = jnp.einsum('tij,tj->ti', precond[:, 0], blocks[1], precision=HIGH) + jnp.einsum('tij,tj->ti', precond[:, 1], blocks[0], precision=HIGH)
    return jnp.stack([real, imag]).reshape(2, -1)

def apply_shift(stiff, vector, mass, shift_pair):
    moved_real = mass * vector[0]
    moved_imag = mass * vector[1]
    real = stiff[0] - (shift_pair[0] * moved_real - shift_pair[1] * moved_imag)
    imag = stiff[1] - (shift_pair[0] * moved_imag + shift_pair[1] * moved_real)
    return jnp.stack([real, imag])

def gram_parts(stack):
    real = jnp.dot(stack[0], stack[0].T, precision=HIGH) + jnp.dot(stack[1], stack[1].T, precision=HIGH)
    imag = jnp.dot(stack[0], stack[1].T, precision=HIGH) - jnp.dot(stack[1], stack[0].T, precision=HIGH)
    return (real, imag)

def minimal_coefficients(gram_real, gram_imag, order):
    top = jnp.concatenate([gram_real[:order, :order], -gram_imag[:order, :order]], axis=1)
    bottom = jnp.concatenate([gram_imag[:order, :order], gram_real[:order, :order]], axis=1)
    system = jnp.concatenate([top, bottom], axis=0)
    target = jnp.concatenate([gram_real[:order, order], gram_imag[:order, order]])
    solved = solve_normal(system, target)
    return (solved[:order], solved[order:])

def operate(vector, shift_pair, k_tiles, pattern, mass, c_tiles, c_rows, c_side, c_count):
    tiles_total = k_tiles.shape[0]
    tile = k_tiles.shape[2]
    group = TD * N_SUB
    blocks = vector.reshape(2, tiles_total, tile)
    ownrow = jnp.arange(tiles_total, dtype=jnp.int32)
    columns = jnp.concatenate([ownrow[:, None], (ownrow // group * group)[:, None] + pattern], axis=1)
    picked = blocks[:, columns]
    stiff = jnp.einsum('tsij,ctsj->cti', k_tiles, picked, precision=HIGH).reshape(2, -1)
    result = apply_shift(stiff, vector, mass, shift_pair)
    slots = jnp.arange(c_tiles.shape[0], dtype=jnp.int32)
    device = slots // CMAX
    within = slots % CMAX
    domain = device // N_SUB
    source_tile = jnp.where(c_side == 0, (device - N_SUB) * TD + TD - 1, (device + N_SUB) * TD)
    present = jnp.where(c_side == 0, domain > 0, domain < N_DOM - 1)
    valid = ((within < c_count[device]) & present).astype(jnp.float32)
    source_tile = jnp.clip(source_tile, 0, tiles_total - 1).astype(jnp.int32)
    contrib = jnp.einsum('sij,csj->csi', c_tiles, blocks[:, source_tile], precision=HIGH) * valid[None, :, None]
    landing = (device * TD + c_rows).astype(jnp.int32)
    extra = jnp.zeros((2, tiles_total, tile), jnp.float32).at[:, landing].add(contrib)
    return result + extra.reshape(2, -1)

def reference(basis, compact, weights, fresh, shifts, k_tiles, pattern, mass, precond, c_tiles, c_rows, c_side, c_count):
    total_rows = basis.shape[2]
    previous = jnp.zeros((2, total_rows), jnp.float32)
    made = []
    listed = []
    for step in range(STEPS):
        beta_real = weights[step, 0]
        beta_imag = weights[step, 1]
        coef_real = jnp.dot(beta_real, compact[0], precision=HIGH) - jnp.dot(beta_imag, compact[1], precision=HIGH)
        coef_imag = jnp.dot(beta_real, compact[1], precision=HIGH) + jnp.dot(beta_imag, compact[0], precision=HIGH)
        gamma_real = jnp.sum(beta_real * fresh[0] - beta_imag * fresh[1])
        gamma_imag = jnp.sum(beta_real * fresh[1] + beta_imag * fresh[0])
        extended = jnp.concatenate([basis, previous[:, None, :]], axis=1)
        right = combine(jnp.concatenate([coef_real, gamma_real[None]]), jnp.concatenate([coef_imag, gamma_imag[None]]), extended)
        terms = [right]
        images = []
        for index in range(ITERS):
            image = operate(precondition(terms[-1], precond), shifts[step], k_tiles, pattern, mass, c_tiles, c_rows, c_side, c_count)
            images.append(image)
            if index + 1 < ITERS:
                terms.append(image - terms[-1])
        stacked = jnp.stack(images + [right], axis=1)
        gram_real, gram_imag = gram_parts(stacked)
        solve_real, solve_imag = minimal_coefficients(gram_real, gram_imag, ITERS)
        direction = combine(solve_real, solve_imag, jnp.stack(terms, axis=1))
        solution = precondition(direction, precond)
        proj_real, proj_imag = conj_products(extended, solution)
        proj_real = proj_real / ROWS
        proj_imag = proj_imag / ROWS
        remain = solution - combine(proj_real, proj_imag, extended)
        norm = jnp.sqrt(jnp.sum(remain * remain) / ROWS + EPSILON)
        latest = remain / norm
        made.append(latest)
        listed.append(jnp.stack([jnp.concatenate([proj_real, norm[None]]), jnp.concatenate([proj_imag, jnp.zeros((1,), jnp.float32)])]))
        previous = latest
    return (jnp.stack(made), jnp.stack(listed))
```

```python
import functools

import jax
import jax.numpy as jnp
from jax import lax
from jax.experimental import pallas as pl
from jax.experimental.pallas import tpu as pltpu
from jax.sharding import PartitionSpec as P

MESH = pl.DeviceIdType.MESH
HIGH = lax.Precision.HIGHEST
F32 = jnp.float32
BF16 = jnp.bfloat16
EPSILON = 1e-06

ITERS = 3
TD = 8
TILE = 128
NB = 16
CORES = 2
Z_CHIPS = 8

PREV, ZROW, UROW, RIGHT, XROWS = 32, 34, 40, 46, 128
NT_DIMS = (((1,), (1,)), ((), ()))


def halves(a):
    hi = a.astype(BF16)
    return hi, (a - hi.astype(F32)).astype(BF16)


def rows4(re, im):
    rh = re.astype(BF16).astype(F32)
    ih = im.astype(BF16).astype(F32)
    return jnp.concatenate([rh, ih, re - rh, im - ih], axis=0).astype(BF16)


def nt(a, b):
    return lax.dot_general(a, b, NT_DIMS, preferred_element_type=F32)


def own_columns(product, lanes):
    lane = lax.broadcasted_iota(jnp.int32, (TILE, lanes), 1) % TD
    total = jnp.zeros((TILE, lanes), F32)
    for t in range(TD):
        total = total + jnp.where(lane == t, product[t * TILE : (t + 1) * TILE], 0.0)
    return total


def fold(columns):
    rows = columns.T
    re, im = rows[0:8], rows[8:16]
    for at in range(16, rows.shape[0], 16):
        re = re + rows[at : at + 8]
        im = im + rows[at + 8 : at + 16]
    return re, im


def gram(top, bottom):
    th, tl = halves(top)
    bh, bl = halves(bottom)
    return nt(jnp.concatenate([th, tl, th, tl], axis=1), jnp.concatenate([bh, bh, bl, bl], axis=1))


def solve(entry):
    def g_re(a, b):
        return entry(2 * a, UROW + 2 * b) + entry(2 * a + 1, UROW + 2 * b + 1)

    def g_im(a, b):
        return entry(2 * a, UROW + 2 * b + 1) - entry(2 * a + 1, UROW + 2 * b)

    real, imag = {}, {}
    for a in range(ITERS):
        for b in range(a + 1):
            real[a, b] = real[b, a] = g_re(a, b)
            if a != b:
                imag[a, b] = g_im(a, b)
                imag[b, a] = -imag[a, b]
            else:
                imag[a, a] = jnp.zeros_like(real[a, a])
    order = 2 * ITERS
    matrix = {}
    for i in range(order):
        for j in range(i + 1):
            a, b = i % ITERS, j % ITERS
            matrix[i, j] = real[a, b] if (i < ITERS) == (j < ITERS) else imag[a, b]
    vector = [g_re(a, ITERS) for a in range(ITERS)] + [g_im(a, ITERS) for a in range(ITERS)]
    lower, inverse = {}, {}
    for i in range(order):
        for j in range(i + 1):
            value = matrix[i, j]
            for k in range(j):
                value = value - lower[i, k] * lower[j, k]
            if i == j:
                inverse[i] = 1.0 / jnp.sqrt(value)
            else:
                lower[i, j] = value * inverse[j]
    forward = []
    for i in range(order):
        value = vector[i]
        for k in range(i):
            value = value - lower[i, k] * forward[k]
        forward.append(value * inverse[i])
    result = [None] * order
    for i in reversed(range(order)):
        value = forward[i]
        for k in range(i + 1, order):
            value = value - lower[k, i] * result[k]
        result[i] = value * inverse[i]
    return result[:ITERS], result[ITERS:]


def kernel(
    sizes,
    pattern,
    c_rows,
    c_side,
    c_count,
    shifts,
    weights,
    compact,
    fresh,
    mass,
    basis,
    k_hbm,
    p_hbm,
    c_hbm,
    made,
    listed,
    k_raw,
    p_raw,
    c_raw,
    k_two,
    p_two,
    c_two,
    stack,
    coef_table,
    weight_rows,
    right_coef,
    basis_gram,
    picked,
    tiles0,
    tiles1,
    tiles2,
    halo,
    sums,
    load_sem,
    tile_send,
    tile_recv,
    halo_send,
    halo_recv,
    sum_send,
    sum_recv,
):
    ny, nz, nc, ns = sizes
    steps = weights.shape[0]
    total_rows = float(ny * nz * nc * ns * TD * TILE)
    n_dom = ny * nz * nc
    dom, sub = lax.axis_index("dom"), lax.axis_index("sub")
    core, chip_z, chip_y = dom % nc, (dom // nc) % nz, dom // (nc * nz)

    def at(y, z, c):
        return (y * nz + z) * nc + c

    def along(stage, d):
        if stage == 0:
            return (dom, (sub + d) % ns)
        if stage == 1:
            return (at((chip_y + d) % ny, chip_z, core), sub)
        if stage == 2:
            return (at(chip_y, (chip_z + d) % nz, core), sub)
        return (at(chip_y, chip_z, (core + d) % nc), sub)

    extents = (ns, ny, nz, nc)
    places = (sub, chip_y, chip_z, core)
    lower_dom, upper_dom = ((dom + n_dom - 1) % n_dom, sub), ((dom + 1) % n_dom, sub)

    loads = [
        pltpu.make_async_copy(basis.at[0], stack.at[pl.ds(0, NB)], load_sem.at[0]),
        pltpu.make_async_copy(basis.at[1], stack.at[pl.ds(NB, NB)], load_sem.at[1]),
        pltpu.make_async_copy(p_hbm, p_raw, load_sem.at[2]),
        pltpu.make_async_copy(k_hbm, k_raw, load_sem.at[3]),
        pltpu.make_async_copy(c_hbm, c_raw, load_sem.at[4]),
    ]
    for load in loads:
        load.start()

    barrier = pltpu.get_barrier_semaphore()
    greeted = 0
    for stage in range(4):
        for d in range(1, extents[stage]):
            pl.semaphore_signal(barrier, inc=1, device_id=along(stage, d), device_id_type=MESH)
            greeted += 1
    for who in (lower_dom, upper_dom):
        pl.semaphore_signal(barrier, inc=1, device_id=who, device_id_type=MESH)
        greeted += 1

    lane = lax.broadcasted_iota(jnp.int32, (8, TILE), 1)
    row = lax.broadcasted_iota(jnp.int32, (8, TILE), 0)

    coef_table[...] = jnp.zeros_like(coef_table)
    terms = compact.shape[1]
    coef_table[0:terms, 0:NB] = compact[0]
    coef_table[0:terms, NB : 2 * NB] = -compact[1]
    coef_table[terms : 2 * terms, 0:NB] = compact[1]
    coef_table[terms : 2 * terms, NB : 2 * NB] = compact[0]
    weight_rows[...] = jnp.zeros_like(weight_rows)
    for k in range(steps):
        weight_rows[2 * k : 2 * k + 1, 0:terms] = weights[k, 0:1, :]
        weight_rows[2 * k : 2 * k + 1, terms : 2 * terms] = -weights[k, 1:2, :]
        weight_rows[2 * k + 1 : 2 * k + 2, 0:terms] = weights[k, 1:2, :]
        weight_rows[2 * k + 1 : 2 * k + 2, terms : 2 * terms] = weights[k, 0:1, :]
    mixed_rows = jnp.dot(
        weight_rows[:, 0 : 2 * terms], coef_table[...], precision=HIGH, preferred_element_type=F32
    )
    for k in range(steps):
        wr, wi = weights[k, 0:1, :], weights[k, 1:2, :]
        fr, fi = fresh[0:1, :], fresh[1:2, :]
        gr = jnp.sum(wr * fr - wi * fi, axis=1, keepdims=True)
        gi = jnp.sum(wr * fi + wi * fr, axis=1, keepdims=True)
        line = lane[0:1]
        first = mixed_rows[2 * k : 2 * k + 1]
        second = mixed_rows[2 * k + 1 : 2 * k + 2]
        first = jnp.where(line == PREV, gr, jnp.where(line == PREV + 1, -gi, first))
        second = jnp.where(line == PREV, gi, jnp.where(line == PREV + 1, gr, second))
        right_coef[k] = jnp.zeros((8, TILE), F32)
        right_coef[k, 0:1, :] = first
        right_coef[k, 1:2, :] = second

    slot_lane = lax.broadcasted_iota(jnp.int32, (1, 64), 1)
    slot_masks = []
    for j in range(TD):
        live = j < c_count[0]
        present = jnp.where(c_side[j] == 0, (dom > 0).astype(jnp.int32), (dom < n_dom - 1).astype(jnp.int32))
        on = jnp.where(live, present, 0)
        hit = (slot_lane // 32 == c_side[j]) & (slot_lane % TD == c_rows[j])
        slot_masks.append(jnp.where(hit, on, 0).astype(F32))

    stack[pl.ds(PREV, XROWS - PREV), :] = jnp.zeros((XROWS - PREV, TD * TILE), F32)
    loads[0].wait()
    loads[1].wait()

    wide = gram(stack[0 : 2 * NB, :], stack[0:XROWS, :])
    basis_gram[...] = jnp.zeros_like(basis_gram)
    basis_gram[:, 0:XROWS] = wide
    upper, under = basis_gram[0:NB, :], basis_gram[NB : 2 * NB, :]
    lane2 = lax.broadcasted_iota(jnp.int32, (NB, TILE), 1)
    mixed = upper + jnp.where(lane2 < NB, pltpu.roll(under, TILE - NB, 1), -pltpu.roll(under, NB, 1))
    mixed = jnp.where(lane2 < 2 * NB, mixed, 0.0)
    basis_part = pltpu.roll(mixed[0:8], 64, 1) + pltpu.roll(mixed[8:16], 96, 1)

    loads[2].wait()

    @pl.loop(0, TD)
    def _(t):
        for c in range(2):
            hi, lo = halves(p_raw[t, c])
            p_two[pl.ds(t * TILE, TILE), (2 * c) * TILE : (2 * c + 1) * TILE] = hi
            p_two[pl.ds(t * TILE, TILE), (2 * c + 1) * TILE : (2 * c + 2) * TILE] = lo

    gathered = (tiles0, tiles1, tiles2)

    def split_rest():
        loads[3].wait()

        @pl.loop(0, TD)
        def _(t):
            for q in range(3):
                hi, lo = halves(k_raw[t, q])
                k_two[pl.ds(t * TILE, TILE), (2 * q) * TILE : (2 * q + 1) * TILE] = hi
                k_two[pl.ds(t * TILE, TILE), (2 * q + 1) * TILE : (2 * q + 2) * TILE] = lo

        loads[4].wait()

        @pl.loop(0, TD)
        def _(t):
            hi, lo = halves(c_raw[t])
            c_two[pl.ds(t * TILE, TILE), 0:TILE] = hi
            c_two[pl.ds(t * TILE, TILE), TILE : 2 * TILE] = lo

    def to_stack(at_row, re, im):
        for t in range(TD):
            stack[at_row : at_row + 1, t * TILE : (t + 1) * TILE] = re[t : t + 1]
            stack[at_row + 1 : at_row + 2, t * TILE : (t + 1) * TILE] = im[t : t + 1]

    def one_step(step):
        right = jnp.dot(
            right_coef[step][:, 0:UROW], stack[0:UROW, :], precision=HIGH, preferred_element_type=F32
        )
        stack[RIGHT : RIGHT + 2, :] = right[0:2]
        t_re = jnp.concatenate([right[0:1, t * TILE : (t + 1) * TILE] for t in range(TD)], axis=0)
        t_im = jnp.concatenate([right[1:2, t * TILE : (t + 1) * TILE] for t in range(TD)], axis=0)
        shift_re, shift_im = shifts[step, 0], shifts[step, 1]
        for it in range(ITERS):
            tiles = gathered[it]
            plain, turned = rows4(t_re, t_im), rows4(-t_im, t_re)
            product = nt(p_two[...], jnp.concatenate([plain, plain, turned, turned], axis=1))
            z_re, z_im = fold(own_columns(product, 32))
            tiles[sub, 0] = z_re
            tiles[sub, 1] = z_im
            if it == 0:

                @pl.when(step == 0)
                def _():
                    pl.semaphore_wait(barrier, greeted)

            copies = []
            for side, who in ((1, lower_dom), (0, upper_dom)):
                copies.append(
                    pltpu.make_async_remote_copy(
                        src_ref=tiles.at[sub],
                        dst_ref=halo.at[step * ITERS + it, side],
                        send_sem=halo_send.at[step * ITERS + it, side],
                        recv_sem=halo_recv.at[step * ITERS + it, side],
                        device_id=who,
                        device_id_type=MESH,
                    )
                )
            for d in range(1, ns):
                copies.append(
                    pltpu.make_async_remote_copy(
                        src_ref=tiles.at[sub],
                        dst_ref=tiles.at[sub],
                        send_sem=tile_send.at[step * ITERS + it, d],
                        recv_sem=tile_recv.at[step * ITERS + it, d],
                        device_id=along(0, d),
                        device_id_type=MESH,
                    )
                )
            for copy in copies:
                copy.start()
            if it == 0:

                @pl.when(step == 0)
                def _():
                    split_rest()

            to_stack(ZROW + 2 * it, z_re, z_im)
            own = rows4(z_re, z_im)
            columns = own_columns(nt(k_two[:, 0 : 2 * TILE], jnp.concatenate([own, own], axis=1)), 32)
            u_re, u_im = fold(columns)
            moved_re, moved_im = mass[...] * z_re, mass[...] * z_im
            u_re = u_re - (shift_re * moved_re - shift_im * moved_im)
            u_im = u_im - (shift_re * moved_im + shift_im * moved_re)

            copies[0].wait_recv()
            copies[1].wait_recv()
            sides = []
            for side, tile in ((0, TD - 1), (1, 0)):
                re = jnp.broadcast_to(halo[step * ITERS + it, side, 0, tile : tile + 1, :], (8, TILE))
                im = jnp.broadcast_to(halo[step * ITERS + it, side, 1, tile : tile + 1, :], (8, TILE))
                sides.append(rows4(re, im))
            rims = jnp.concatenate(sides, axis=0)
            product = nt(c_two[...], jnp.concatenate([rims, rims], axis=1))
            columns = jnp.zeros((TILE, 64), F32)
            for j in range(TD):
                columns = columns + slot_masks[j] * product[j * TILE : (j + 1) * TILE]
            c_re, c_im = fold(columns)
            u_re, u_im = u_re + c_re, u_im + c_im

            for copy in copies[2:]:
                copy.wait_recv()
            for q in range(2):
                for t in range(TD):
                    source = pattern[t, q]
                    for c in range(2):
                        picked[q, c, t : t + 1, :] = tiles[source // TD, c, pl.ds(source % TD, 1), :]
            first = rows4(picked[0, 0], picked[0, 1])
            second = rows4(picked[1, 0], picked[1, 1])
            product = nt(k_two[:, 2 * TILE :], jnp.concatenate([first, first, second, second], axis=1))
            k_re, k_im = fold(own_columns(product, 32))
            u_re, u_im = u_re + k_re, u_im + k_im
            to_stack(UROW + 2 * it, u_re, u_im)
            t_re, t_im = u_re - t_re, u_im - t_im
            for copy in copies:
                copy.wait_send()

        both = gram(stack[PREV:48, :], stack[0:XROWS, :])
        narrow = lax.broadcasted_iota(jnp.int32, (8, XROWS), 1)
        sums[step, 0, sub] = basis_part
        sums[step, 0, sub] = jnp.where(narrow < UROW, both[0:8], jnp.where(narrow < 48, both[8:16], basis_part))
        for stage in range(4):
            place = places[stage]
            copies = []
            for d in range(1, extents[stage]):
                copies.append(
                    pltpu.make_async_remote_copy(
                        src_ref=sums.at[step, stage, place],
                        dst_ref=sums.at[step, stage, place],
                        send_sem=sum_send.at[step, stage, d],
                        recv_sem=sum_recv.at[step, stage, d],
                        device_id=along(stage, d),
                        device_id_type=MESH,
                    )
                )
            for copy in copies:
                copy.start()
            for copy in copies:
                copy.wait_recv()
            reduced = sums[step, stage, 0]
            for other in range(1, extents[stage]):
                reduced = reduced + sums[step, stage, other]
            if stage < 3:
                sums[step, stage + 1, places[stage + 1]] = reduced
            for copy in copies:
                copy.wait_send()

        def entry(i, j):
            return jnp.broadcast_to(reduced[i : i + 1, j : j + 1], (8, TILE))

        def line_of(i):
            return jnp.broadcast_to(reduced[i : i + 1, :], (8, TILE))

        y_re, y_im = solve(entry)
        with_re = jnp.zeros((8, TILE), F32)
        with_im = jnp.zeros((8, TILE), F32)
        sol_re = jnp.zeros((8, TILE), F32)
        sol_im = jnp.zeros((8, TILE), F32)
        for j in range(ITERS):
            a, b = line_of(2 + 2 * j), line_of(3 + 2 * j)
            with_re = with_re + (y_re[j] * a - y_im[j] * b)
            with_im = with_im + (y_re[j] * b + y_im[j] * a)
            here, after = lane == ZROW + 2 * j, lane == ZROW + 2 * j + 1
            sol_re = jnp.where(here, y_re[j], jnp.where(after, -y_im[j], sol_re))
            sol_im = jnp.where(here, y_im[j], jnp.where(after, y_re[j], sol_im))

        def back(a, n):
            return pltpu.roll(a, TILE - n, 1)

        on_basis, on_prev = lane < NB, lane == PREV
        h_re = jnp.where(
            on_basis, with_re + back(with_im, NB), jnp.where(on_prev, with_re + back(with_im, 1), 0.0)
        )
        h_im = jnp.where(
            on_basis, with_im - back(with_re, NB), jnp.where(on_prev, with_im - back(with_re, 1), 0.0)
        )
        h_re, h_im = h_re / total_rows, h_im / total_rows
        on_imag, on_prev_imag = (lane >= NB) & (lane < 2 * NB), lane == PREV + 1
        e_re = h_re - jnp.where(
            on_imag, pltpu.roll(h_im, NB, 1), jnp.where(on_prev_imag, pltpu.roll(h_im, 1, 1), 0.0)
        )
        e_im = h_im + jnp.where(
            on_imag, pltpu.roll(h_re, NB, 1), jnp.where(on_prev_imag, pltpu.roll(h_re, 1, 1), 0.0)
        )

        @pl.when(step == 0)
        def _():
            basis_gram[0:8, :] = jnp.where(lane < 2 * NB, pltpu.roll(reduced, 64, 1), 0.0)
            basis_gram[8:16, :] = jnp.where(lane < 2 * NB, pltpu.roll(reduced, 32, 1), 0.0)

        pair = jnp.where(row == 0, e_re, jnp.where(row == 1, e_im, 0.0))
        turned = jnp.dot(pair[:, 0:NB], basis_gram[0:NB, :], precision=HIGH, preferred_element_type=F32)
        p_re = jnp.broadcast_to(h_re[0:1, PREV : PREV + 1], (8, TILE))
        p_im = jnp.broadcast_to(h_im[0:1, PREV : PREV + 1], (8, TILE))
        prev_re, prev_im = line_of(0), line_of(1)
        v_re, v_im = p_re * prev_re - p_im * prev_im, p_im * prev_re + p_re * prev_im
        share = jnp.where(lane < PREV, 2.0, jnp.where(lane < PREV + 2, 1.0, 0.0))
        first_row = (
            sol_re * with_re
            + sol_im * with_im
            - 2.0 * total_rows * (h_re * h_re + h_im * h_im)
            + share * (v_re * e_re + v_im * e_im)
        )
        first_row = jnp.where(lane < UROW, first_row, 0.0)
        each = turned * pair + jnp.where(row == 0, first_row, 0.0)
        squares = jnp.sum(jnp.sum(each, axis=0, keepdims=True), axis=1, keepdims=True)
        squares = jnp.broadcast_to(squares, (8, TILE))
        norm = jnp.sqrt(jnp.maximum(squares, 0.0) / total_rows + EPSILON)

        coef = jnp.where(row == 0, sol_re - e_re, jnp.where(row == 1, sol_im - e_im, 0.0)) / norm
        latest = jnp.dot(coef[:, 0:UROW], stack[0:UROW, :], precision=HIGH, preferred_element_type=F32)
        made[step] = latest[0:2]
        stack[PREV : PREV + 2, :] = latest[0:2]
        top = jnp.where(on_basis, h_re, jnp.where(lane == NB, back(h_re, NB), norm))
        low = jnp.where(on_basis, h_im, jnp.where(lane == NB, back(h_im, NB), 0.0))
        listed[step, 0:1, :] = top[0:1, 0 : NB + 2]
        listed[step, 1:2, :] = low[0:1, 0 : NB + 2]

    @pl.loop(0, steps)
    def _(step):
        one_step(step)


def solution(mesh, y_chips=None):
    ns, n_dom = mesh.shape["sub"], mesh.shape["dom"]
    nz = Z_CHIPS if y_chips is None else n_dom // CORES // y_chips
    sizes = (n_dom // (CORES * nz), nz, CORES, ns)
    most = max(sizes)

    def local(basis, compact, weights, fresh, shifts, k_tiles, pattern, mass, precond, c_tiles, c_rows, c_side, c_count):
        smem = pl.BlockSpec(memory_space=pltpu.SMEM)
        vmem = pl.BlockSpec(memory_space=pltpu.VMEM)
        anywhere = pl.BlockSpec(memory_space=pl.ANY)
        steps = weights.shape[0]
        rows = TD * TILE
        return pl.pallas_call(
            functools.partial(kernel, sizes),
            out_shape=(
                jax.ShapeDtypeStruct((steps, 2, rows), F32),
                jax.ShapeDtypeStruct((steps, 2, NB + 2), F32),
            ),
            in_specs=[smem] * 5 + [vmem] * 4 + [anywhere] * 4,
            out_specs=(vmem, vmem),
            scratch_shapes=[
                pltpu.VMEM((TD, 3, TILE, TILE), F32),
                pltpu.VMEM((TD, 2, TILE, TILE), F32),
                pltpu.VMEM((TD, TILE, TILE), F32),
                pltpu.VMEM((rows, 6 * TILE), BF16),
                pltpu.VMEM((rows, 4 * TILE), BF16),
                pltpu.VMEM((rows, 2 * TILE), BF16),
                pltpu.VMEM((XROWS, rows), F32),
                pltpu.VMEM((2 * weights.shape[2], TILE), F32),
                pltpu.VMEM((8, TILE), F32),
                pltpu.VMEM((steps, 8, TILE), F32),
                pltpu.VMEM((2 * NB, TILE), F32),
                pltpu.VMEM((2, 2, TD, TILE), F32),
                pltpu.VMEM((ns, 2, TD, TILE), F32),
                pltpu.VMEM((ns, 2, TD, TILE), F32),
                pltpu.VMEM((ns, 2, TD, TILE), F32),
                pltpu.VMEM((steps * ITERS, 2, 2, TD, TILE), F32),
                pltpu.VMEM((steps, 4, most, 8, TILE), F32),
                pltpu.SemaphoreType.DMA((5,)),
                pltpu.SemaphoreType.DMA((steps * ITERS, ns)),
                pltpu.SemaphoreType.DMA((steps * ITERS, ns)),
                pltpu.SemaphoreType.DMA((steps * ITERS, 2)),
                pltpu.SemaphoreType.DMA((steps * ITERS, 2)),
                pltpu.SemaphoreType.DMA((steps, 4, most)),
                pltpu.SemaphoreType.DMA((steps, 4, most)),
            ],
            compiler_params=pltpu.CompilerParams(collective_id=0, has_side_effects=True),
        )(
            pattern,
            c_rows,
            c_side,
            c_count,
            shifts,
            weights,
            compact,
            fresh,
            mass.reshape(TD, TILE),
            basis,
            k_tiles,
            precond,
            c_tiles,
        )

    both = ("dom", "sub")
    placed = (
        P(None, None, both),
        P(),
        P(),
        P(),
        P(),
        P(both, None, None, None),
        P(both, None),
        P(both),
        P(both, None, None, None),
        P(both, None, None),
        P(both),
        P(both),
        P(both),
    )
    return jax.shard_map(
        local, mesh=mesh, in_specs=placed, out_specs=(P(None, None, both), P()), check_vma=False
    )
```

```python
import functools

import jax
import jax.numpy as jnp
from jax import lax
from jax.experimental import pallas as pl
from jax.experimental.pallas import tpu as pltpu
from jax.sharding import PartitionSpec as P

MESH = pl.DeviceIdType.MESH
HIGH = lax.Precision.HIGHEST
F32 = jnp.float32
BF16 = jnp.bfloat16
EPSILON = 1e-06

ITERS = 3
TD = 8
TILE = 128
NB = 16
CORES = 2
Z_CHIPS = 8

PREV, ZROW, UROW, RIGHT, XROWS = 32, 34, 40, 46, 128
NT_DIMS = (((1,), (1,)), ((), ()))


def halves(a):
    hi = a.astype(BF16)
    return hi, (a - hi.astype(F32)).astype(BF16)


def rows4(re, im):
    rh = re.astype(BF16).astype(F32)
    ih = im.astype(BF16).astype(F32)
    return jnp.concatenate([rh, ih, re - rh, im - ih], axis=0).astype(BF16)


def nt(a, b):
    return lax.dot_general(a, b, NT_DIMS, preferred_element_type=F32)


def own_columns(product, lanes):
    lane = lax.broadcasted_iota(jnp.int32, (TILE, lanes), 1) % TD
    total = jnp.zeros((TILE, lanes), F32)
    for t in range(TD):
        total = total + jnp.where(lane == t, product[t * TILE : (t + 1) * TILE], 0.0)
    return total


def fold(columns):
    rows = columns.T
    re, im = rows[0:8], rows[8:16]
    for at in range(16, rows.shape[0], 16):
        re = re + rows[at : at + 8]
        im = im + rows[at + 8 : at + 16]
    return re, im


def gram(top, bottom):
    th, tl = halves(top)
    bh, bl = halves(bottom)
    return nt(jnp.concatenate([th, tl, th, tl], axis=1), jnp.concatenate([bh, bh, bl, bl], axis=1))


def solve(entry):
    def g_re(a, b):
        return entry(2 * a, UROW + 2 * b) + entry(2 * a + 1, UROW + 2 * b + 1)

    def g_im(a, b):
        return entry(2 * a, UROW + 2 * b + 1) - entry(2 * a + 1, UROW + 2 * b)

    real, imag = {}, {}
    for a in range(ITERS):
        for b in range(a + 1):
            real[a, b] = real[b, a] = g_re(a, b)
            if a != b:
                imag[a, b] = g_im(a, b)
                imag[b, a] = -imag[a, b]
            else:
                imag[a, a] = jnp.zeros_like(real[a, a])
    order = 2 * ITERS
    matrix = {}
    for i in range(order):
        for j in range(i + 1):
            a, b = i % ITERS, j % ITERS
            matrix[i, j] = real[a, b] if (i < ITERS) == (j < ITERS) else imag[a, b]
    vector = [g_re(a, ITERS) for a in range(ITERS)] + [g_im(a, ITERS) for a in range(ITERS)]
    lower, inverse = {}, {}
    for i in range(order):
        for j in range(i + 1):
            value = matrix[i, j]
            for k in range(j):
                value = value - lower[i, k] * lower[j, k]
            if i == j:
                inverse[i] = 1.0 / jnp.sqrt(value)
            else:
                lower[i, j] = value * inverse[j]
    forward = []
    for i in range(order):
        value = vector[i]
        for k in range(i):
            value = value - lower[i, k] * forward[k]
        forward.append(value * inverse[i])
    result = [None] * order
    for i in reversed(range(order)):
        value = forward[i]
        for k in range(i + 1, order):
            value = value - lower[k, i] * result[k]
        result[i] = value * inverse[i]
    return result[:ITERS], result[ITERS:]


def kernel(
    sizes,
    pattern,
    c_rows,
    c_side,
    c_count,
    shifts,
    weights,
    compact,
    fresh,
    mass,
    basis,
    k_hbm,
    p_hbm,
    c_hbm,
    made,
    listed,
    k_raw,
    p_raw,
    c_raw,
    k_two,
    p_two,
    c_two,
    stack,
    coef_table,
    weight_rows,
    right_coef,
    basis_gram,
    picked,
    tiles0,
    tiles1,
    tiles2,
    halo,
    sums,
    basis_sums,
    slot_masks,
    load_sem,
    tile_send,
    tile_recv,
    halo_send,
    halo_recv,
    sum_send,
    sum_recv,
    basis_send,
    basis_recv,
):
    ny, nz, nc, ns = sizes
    steps = weights.shape[0]
    total_rows = float(ny * nz * nc * ns * TD * TILE)
    n_dom = ny * nz * nc
    dom, sub = lax.axis_index("dom"), lax.axis_index("sub")
    core, chip_z, chip_y = dom % nc, (dom // nc) % nz, dom // (nc * nz)

    def at(y, z, c):
        return (y * nz + z) * nc + c

    def along(stage, d):
        if stage == 0:
            return (dom, (sub + d) % ns)
        if stage == 1:
            return (at((chip_y + d) % ny, chip_z, core), sub)
        return (at(chip_y, (chip_z + d // nc) % nz, (core + d) % nc), sub)

    extents = (ns, ny, nz * nc)
    places = (sub, chip_y, chip_z * nc + core)
    stages = len(extents)

    def send_sum(store, prefix, send_sem, recv_sem, stage):
        mine = store.at[(*prefix, stage, places[stage])]
        for d in range(1, extents[stage]):
            pltpu.make_async_remote_copy(
                src_ref=mine,
                dst_ref=mine,
                send_sem=send_sem.at[(*prefix, stage)],
                recv_sem=recv_sem.at[(*prefix, stage)],
                device_id=along(stage, d),
                device_id_type=MESH,
            ).start()

    def wait_for(ref, sem):
        pltpu.make_async_copy(ref, ref, sem).wait()

    def finish_sum(store, prefix, send_sem, recv_sem, stage):
        others = store.at[(*prefix, stage, pl.ds(0, extents[stage] - 1))]
        wait_for(others, recv_sem.at[(*prefix, stage)])
        total = store[(*prefix, stage, 0)]
        for other in range(1, extents[stage]):
            total = total + store[(*prefix, stage, other)]
        wait_for(others, send_sem.at[(*prefix, stage)])
        return total
    lower_dom, upper_dom = ((dom + n_dom - 1) % n_dom, sub), ((dom + 1) % n_dom, sub)

    loads = [
        pltpu.make_async_copy(basis.at[0], stack.at[pl.ds(0, NB)], load_sem.at[0]),
        pltpu.make_async_copy(basis.at[1], stack.at[pl.ds(NB, NB)], load_sem.at[1]),
        pltpu.make_async_copy(p_hbm, p_raw, load_sem.at[2]),
        pltpu.make_async_copy(k_hbm, k_raw, load_sem.at[3]),
        pltpu.make_async_copy(c_hbm, c_raw, load_sem.at[4]),
    ]
    for load in loads:
        load.start()

    barrier = pltpu.get_barrier_semaphore()
    greeted = 0
    for stage in range(stages):
        for d in range(1, extents[stage]):
            pl.semaphore_signal(barrier, inc=1, device_id=along(stage, d), device_id_type=MESH)
            greeted += 1
    for who in (lower_dom, upper_dom):
        pl.semaphore_signal(barrier, inc=1, device_id=who, device_id_type=MESH)
        greeted += 1

    lane = lax.broadcasted_iota(jnp.int32, (8, TILE), 1)
    row = lax.broadcasted_iota(jnp.int32, (8, TILE), 0)
    lane2 = lax.broadcasted_iota(jnp.int32, (NB, TILE), 1)

    terms = weights.shape[2]
    coef_table[...] = jnp.zeros_like(coef_table)
    coef_table[0:NB, 0:terms] = compact[0]
    coef_table[0:NB, terms : 2 * terms] = compact[1]
    coef_table[NB : 2 * NB, 0:terms] = -compact[1]
    coef_table[NB : 2 * NB, terms : 2 * terms] = compact[0]
    weight_rows[...] = jnp.zeros_like(weight_rows)
    for k in range(steps):
        weight_rows[2 * k : 2 * k + 1, 0:terms] = weights[k, 0:1, :]
        weight_rows[2 * k : 2 * k + 1, terms : 2 * terms] = -weights[k, 1:2, :]
        weight_rows[2 * k + 1 : 2 * k + 2, 0:terms] = weights[k, 1:2, :]
        weight_rows[2 * k + 1 : 2 * k + 2, terms : 2 * terms] = weights[k, 0:1, :]
    mixed_rows = lax.dot_general(
        weight_rows[...], coef_table[...], NT_DIMS, precision=HIGH, preferred_element_type=F32
    )
    for k in range(steps):
        wr, wi = weights[k, 0:1, :], weights[k, 1:2, :]
        fr, fi = fresh[0:1, :], fresh[1:2, :]
        gr = jnp.sum(wr * fr - wi * fi, axis=1, keepdims=True)
        gi = jnp.sum(wr * fi + wi * fr, axis=1, keepdims=True)
        line = lane[0:1]
        first = mixed_rows[2 * k : 2 * k + 1]
        second = mixed_rows[2 * k + 1 : 2 * k + 2]
        first = jnp.where(line == PREV, gr, jnp.where(line == PREV + 1, -gi, first))
        second = jnp.where(line == PREV, gi, jnp.where(line == PREV + 1, gr, second))
        right_coef[k] = jnp.zeros((8, TILE), F32)
        right_coef[k, 0:1, :] = first
        right_coef[k, 1:2, :] = second

    stack[pl.ds(PREV, 16), :] = jnp.zeros((16, TD * TILE), F32)
    loads[0].wait()
    loads[1].wait()

    loads[2].wait()

    @pl.loop(0, TD)
    def _(t):
        for c in range(2):
            hi, lo = halves(p_raw[t, c])
            p_two[pl.ds(t * TILE, TILE), (2 * c) * TILE : (2 * c + 1) * TILE] = hi
            p_two[pl.ds(t * TILE, TILE), (2 * c + 1) * TILE : (2 * c + 2) * TILE] = lo

    gathered = (tiles0, tiles1, tiles2)

    def late_start():
        slot_lane = lax.broadcasted_iota(jnp.int32, (1, 64), 1)
        for j in range(TD):
            live = j < c_count[0]
            present = jnp.where(c_side[j] == 0, (dom > 0).astype(jnp.int32), (dom < n_dom - 1).astype(jnp.int32))
            on = jnp.where(live, present, 0)
            hit = (slot_lane // 32 == c_side[j]) & (slot_lane % TD == c_rows[j])
            slot_masks[j : j + 1, :] = jnp.where(hit, on, 0).astype(F32)

        stack[pl.ds(PREV + 16, XROWS - PREV - 16), :] = jnp.zeros((XROWS - PREV - 16, TD * TILE), F32)
        wide = gram(stack[0 : 2 * NB, :], stack[0:XROWS, :])
        basis_gram[...] = jnp.zeros_like(basis_gram)
        basis_gram[:, 0:XROWS] = wide
        upper, under = basis_gram[0:NB, :], basis_gram[NB : 2 * NB, :]
        mixed = upper + jnp.where(lane2 < NB, pltpu.roll(under, TILE - NB, 1), -pltpu.roll(under, NB, 1))
        mixed = jnp.where(lane2 < 2 * NB, mixed, 0.0)
        basis_part = (
            mixed[0:4] + pltpu.roll(mixed[4:8], 32, 1) + pltpu.roll(mixed[8:12], 64, 1) + pltpu.roll(mixed[12:16], 96, 1)
        )
        basis_sums[0, places[0]] = basis_part

        send_sum(basis_sums, (), basis_send, basis_recv, 0)

    def split_rest():
        loads[3].wait()

        @pl.loop(0, TD)
        def _(t):
            for q in range(3):
                hi, lo = halves(k_raw[t, q])
                k_two[pl.ds(t * TILE, TILE), (2 * q) * TILE : (2 * q + 1) * TILE] = hi
                k_two[pl.ds(t * TILE, TILE), (2 * q + 1) * TILE : (2 * q + 2) * TILE] = lo

        loads[4].wait()

        @pl.loop(0, TD)
        def _(t):
            hi, lo = halves(c_raw[t])
            c_two[pl.ds(t * TILE, TILE), 0:TILE] = hi
            c_two[pl.ds(t * TILE, TILE), TILE : 2 * TILE] = lo

    def to_stack(at_row, re, im):
        for t in range(TD):
            stack[at_row : at_row + 1, t * TILE : (t + 1) * TILE] = re[t : t + 1]
            stack[at_row + 1 : at_row + 2, t * TILE : (t + 1) * TILE] = im[t : t + 1]

    def one_step(step):
        right = jnp.dot(
            right_coef[step][:, 0:UROW], stack[0:UROW, :], precision=HIGH, preferred_element_type=F32
        )
        stack[RIGHT : RIGHT + 2, :] = right[0:2]
        t_re = jnp.concatenate([right[0:1, t * TILE : (t + 1) * TILE] for t in range(TD)], axis=0)
        t_im = jnp.concatenate([right[1:2, t * TILE : (t + 1) * TILE] for t in range(TD)], axis=0)
        shift_re, shift_im = shifts[step, 0], shifts[step, 1]
        for it in range(ITERS):
            tiles = gathered[it]
            plain, turned = rows4(t_re, t_im), rows4(-t_im, t_re)
            product = nt(p_two[...], jnp.concatenate([plain, plain, turned, turned], axis=1))
            z_re, z_im = fold(own_columns(product, 32))
            tiles[sub, 0] = z_re
            tiles[sub, 1] = z_im
            if it == 0:

                @pl.when(step == 0)
                def _():
                    pl.semaphore_wait(barrier, greeted)

            turn = step * ITERS + it
            for side, who in ((1, lower_dom), (0, upper_dom)):
                pltpu.make_async_remote_copy(
                    src_ref=tiles.at[sub],
                    dst_ref=halo.at[turn, side],
                    send_sem=halo_send.at[turn],
                    recv_sem=halo_recv.at[turn],
                    device_id=who,
                    device_id_type=MESH,
                ).start()
            for d in range(1, ns):
                pltpu.make_async_remote_copy(
                    src_ref=tiles.at[sub],
                    dst_ref=tiles.at[sub],
                    send_sem=tile_send.at[turn],
                    recv_sem=tile_recv.at[turn],
                    device_id=along(0, d),
                    device_id_type=MESH,
                ).start()
            if it == 0:

                @pl.when(step == 0)
                def _():
                    split_rest()
                    late_start()

            else:

                @pl.when(step == 0)
                def _():
                    so_far = finish_sum(basis_sums, (), basis_send, basis_recv, it - 1)
                    basis_sums[it, places[it]] = so_far
                    send_sum(basis_sums, (), basis_send, basis_recv, it)

            to_stack(ZROW + 2 * it, z_re, z_im)
            own = rows4(z_re, z_im)
            columns = own_columns(nt(k_two[:, 0 : 2 * TILE], jnp.concatenate([own, own], axis=1)), 32)
            u_re, u_im = fold(columns)
            moved_re, moved_im = mass[...] * z_re, mass[...] * z_im
            u_re = u_re - (shift_re * moved_re - shift_im * moved_im)
            u_im = u_im - (shift_re * moved_im + shift_im * moved_re)

            wait_for(halo.at[turn], halo_recv.at[turn])
            sides = []
            for side, tile in ((0, TD - 1), (1, 0)):
                re = jnp.broadcast_to(halo[turn, side, 0, tile : tile + 1, :], (8, TILE))
                im = jnp.broadcast_to(halo[turn, side, 1, tile : tile + 1, :], (8, TILE))
                sides.append(rows4(re, im))
            rims = jnp.concatenate(sides, axis=0)
            product = nt(c_two[...], jnp.concatenate([rims, rims], axis=1))
            columns = jnp.zeros((TILE, 64), F32)
            for j in range(TD):
                columns = columns + slot_masks[j : j + 1, :] * product[j * TILE : (j + 1) * TILE]
            c_re, c_im = fold(columns)
            u_re, u_im = u_re + c_re, u_im + c_im

            wait_for(tiles.at[pl.ds(0, ns - 1)], tile_recv.at[turn])
            for q in range(2):
                for t in range(TD):
                    source = pattern[q, t]
                    for c in range(2):
                        picked[q, c, t : t + 1, :] = tiles[source // TD, c, pl.ds(source % TD, 1), :]
            first = rows4(picked[0, 0], picked[0, 1])
            second = rows4(picked[1, 0], picked[1, 1])
            product = nt(k_two[:, 2 * TILE :], jnp.concatenate([first, first, second, second], axis=1))
            k_re, k_im = fold(own_columns(product, 32))
            u_re, u_im = u_re + k_re, u_im + k_im
            to_stack(UROW + 2 * it, u_re, u_im)
            t_re, t_im = u_re - t_re, u_im - t_im
            wait_for(halo.at[turn], halo_send.at[turn])
            wait_for(tiles.at[pl.ds(0, ns - 1)], tile_send.at[turn])

        both = gram(stack[PREV:48, :], stack[0:XROWS, :])
        packed = jnp.where(lane < UROW, both[0:8], jnp.where(lane < RIGHT + 2, both[8:16], 0.0))
        part = packed[0:4] + pltpu.roll(packed[4:8], 64, 1)
        for stage in range(stages):
            sums[step, stage, places[stage]] = part
            send_sum(sums, (step,), sum_send, sum_recv, stage)
            part = finish_sum(sums, (step,), sum_send, sum_recv, stage)
        reduced = jnp.concatenate([part, pltpu.roll(part, 64, 1)], axis=0)

        def entry(i, j):
            return jnp.broadcast_to(reduced[i : i + 1, j : j + 1], (8, TILE))

        def line_of(i):
            return jnp.broadcast_to(reduced[i : i + 1, :], (8, TILE))

        y_re, y_im = solve(entry)
        with_re = jnp.zeros((8, TILE), F32)
        with_im = jnp.zeros((8, TILE), F32)
        sol_re = jnp.zeros((8, TILE), F32)
        sol_im = jnp.zeros((8, TILE), F32)
        for j in range(ITERS):
            a, b = line_of(2 + 2 * j), line_of(3 + 2 * j)
            with_re = with_re + (y_re[j] * a - y_im[j] * b)
            with_im = with_im + (y_re[j] * b + y_im[j] * a)
            here, after = lane == ZROW + 2 * j, lane == ZROW + 2 * j + 1
            sol_re = jnp.where(here, y_re[j], jnp.where(after, -y_im[j], sol_re))
            sol_im = jnp.where(here, y_im[j], jnp.where(after, y_re[j], sol_im))

        def back(a, n):
            return pltpu.roll(a, TILE - n, 1)

        on_basis, on_prev = lane < NB, lane == PREV
        h_re = jnp.where(
            on_basis, with_re + back(with_im, NB), jnp.where(on_prev, with_re + back(with_im, 1), 0.0)
        )
        h_im = jnp.where(
            on_basis, with_im - back(with_re, NB), jnp.where(on_prev, with_im - back(with_re, 1), 0.0)
        )
        h_re, h_im = h_re / total_rows, h_im / total_rows
        on_imag, on_prev_imag = (lane >= NB) & (lane < 2 * NB), lane == PREV + 1
        e_re = h_re - jnp.where(
            on_imag, pltpu.roll(h_im, NB, 1), jnp.where(on_prev_imag, pltpu.roll(h_im, 1, 1), 0.0)
        )
        e_im = h_im + jnp.where(
            on_imag, pltpu.roll(h_re, NB, 1), jnp.where(on_prev_imag, pltpu.roll(h_re, 1, 1), 0.0)
        )

        @pl.when(step == 0)
        def _():
            whole = finish_sum(basis_sums, (), basis_send, basis_recv, stages - 1)
            blocks = [whole] + [pltpu.roll(whole, TILE - shift, 1) for shift in (32, 64, 96)]
            basis_gram[0:NB, :] = jnp.where(lane2 < 2 * NB, jnp.concatenate(blocks, axis=0), 0.0)

        pair = jnp.where(row == 0, e_re, jnp.where(row == 1, e_im, 0.0))
        turned = jnp.dot(pair[:, 0:NB], basis_gram[0:NB, :], precision=HIGH, preferred_element_type=F32)
        p_re = jnp.broadcast_to(h_re[0:1, PREV : PREV + 1], (8, TILE))
        p_im = jnp.broadcast_to(h_im[0:1, PREV : PREV + 1], (8, TILE))
        prev_re, prev_im = line_of(0), line_of(1)
        v_re, v_im = p_re * prev_re - p_im * prev_im, p_im * prev_re + p_re * prev_im
        share = jnp.where(lane < PREV, 2.0, jnp.where(lane < PREV + 2, 1.0, 0.0))
        first_row = (
            sol_re * with_re
            + sol_im * with_im
            - 2.0 * total_rows * (h_re * h_re + h_im * h_im)
            + share * (v_re * e_re + v_im * e_im)
        )
        first_row = jnp.where(lane < UROW, first_row, 0.0)
        each = turned * pair + jnp.where(row == 0, first_row, 0.0)
        squares = jnp.sum(jnp.sum(each, axis=0, keepdims=True), axis=1, keepdims=True)
        squares = jnp.broadcast_to(squares, (8, TILE))
        norm = jnp.sqrt(jnp.maximum(squares, 0.0) / total_rows + EPSILON)

        coef = jnp.where(row == 0, sol_re - e_re, jnp.where(row == 1, sol_im - e_im, 0.0)) / norm
        latest = jnp.dot(coef[:, 0:UROW], stack[0:UROW, :], precision=HIGH, preferred_element_type=F32)
        made[step] = latest[0:2]
        stack[PREV : PREV + 2, :] = latest[0:2]
        top = jnp.where(on_basis, h_re, jnp.where(lane == NB, back(h_re, NB), norm))
        low = jnp.where(on_basis, h_im, jnp.where(lane == NB, back(h_im, NB), 0.0))
        listed[step, 0:1, :] = top[0:1, 0 : NB + 2]
        listed[step, 1:2, :] = low[0:1, 0 : NB + 2]

    @pl.loop(0, steps)
    def _(step):
        one_step(step)


def solution(mesh, y_chips=None):
    ns, n_dom = mesh.shape["sub"], mesh.shape["dom"]
    nz = Z_CHIPS if y_chips is None else n_dom // CORES // y_chips
    sizes = (n_dom // (CORES * nz), nz, CORES, ns)
    most = max(ns, sizes[0], nz * CORES)

    def local(basis, compact, weights, fresh, shifts, k_tiles, pattern, mass, precond, c_tiles, c_rows, c_side, c_count):
        smem = pl.BlockSpec(memory_space=pltpu.SMEM)
        vmem = pl.BlockSpec(memory_space=pltpu.VMEM)
        anywhere = pl.BlockSpec(memory_space=pl.ANY)
        steps = weights.shape[0]
        rows = TD * TILE
        return pl.pallas_call(
            functools.partial(kernel, sizes),
            out_shape=(
                jax.ShapeDtypeStruct((steps, 2, rows), F32),
                jax.ShapeDtypeStruct((steps, 2, NB + 2), F32),
            ),
            in_specs=[smem] * 5 + [vmem] * 4 + [anywhere] * 4,
            out_specs=(vmem, vmem),
            scratch_shapes=[
                pltpu.VMEM((TD, 3, TILE, TILE), F32),
                pltpu.VMEM((TD, 2, TILE, TILE), F32),
                pltpu.VMEM((TD, TILE, TILE), F32),
                pltpu.VMEM((rows, 6 * TILE), BF16),
                pltpu.VMEM((rows, 4 * TILE), BF16),
                pltpu.VMEM((rows, 2 * TILE), BF16),
                pltpu.VMEM((XROWS, rows), F32),
                pltpu.VMEM((TILE, TILE), F32),
                pltpu.VMEM((8, TILE), F32),
                pltpu.VMEM((steps, 8, TILE), F32),
                pltpu.VMEM((2 * NB, TILE), F32),
                pltpu.VMEM((2, 2, TD, TILE), F32),
                pltpu.VMEM((ns, 2, TD, TILE), F32),
                pltpu.VMEM((ns, 2, TD, TILE), F32),
                pltpu.VMEM((ns, 2, TD, TILE), F32),
                pltpu.VMEM((steps * ITERS, 2, 2, TD, TILE), F32),
                pltpu.VMEM((steps, 3, most, 4, TILE), F32),
                pltpu.VMEM((3, most, 4, TILE), F32),
                pltpu.VMEM((TD, 64), F32),
                pltpu.SemaphoreType.DMA((5,)),
                pltpu.SemaphoreType.DMA((steps * ITERS,)),
                pltpu.SemaphoreType.DMA((steps * ITERS,)),
                pltpu.SemaphoreType.DMA((steps * ITERS,)),
                pltpu.SemaphoreType.DMA((steps * ITERS,)),
                pltpu.SemaphoreType.DMA((steps, 3)),
                pltpu.SemaphoreType.DMA((steps, 3)),
                pltpu.SemaphoreType.DMA((3,)),
                pltpu.SemaphoreType.DMA((3,)),
            ],
            compiler_params=pltpu.CompilerParams(collective_id=0, has_side_effects=True),
        )(
            pattern.T,
            c_rows,
            c_side,
            c_count,
            shifts,
            weights,
            jnp.swapaxes(compact, 1, 2),
            fresh,
            mass.reshape(TD, TILE),
            basis,
            k_tiles,
            precond,
            c_tiles,
        )

    both = ("dom", "sub")
    placed = (
        P(None, None, both),
        P(),
        P(),
        P(),
        P(),
        P(both, None, None, None),
        P(both, None),
        P(both),
        P(both, None, None, None),
        P(both, None, None),
        P(both),
        P(both),
        P(both),
    )
    return jax.shard_map(
        local, mesh=mesh, in_specs=placed, out_specs=(P(None, None, both), P()), check_vma=False
    )
```

```python
import functools

import jax
import jax.numpy as jnp
from jax import lax
from jax.experimental import pallas as pl
from jax.experimental.pallas import tpu as pltpu
from jax.sharding import PartitionSpec as P

MESH = pl.DeviceIdType.MESH
HIGH = lax.Precision.HIGHEST
F32 = jnp.float32
BF16 = jnp.bfloat16
EPSILON = 1e-06

ITERS = 3
TD = 8
TILE = 128
NB = 16
CORES = 2
Z_CHIPS = 8

PREV, ZROW, UROW, RIGHT, XROWS = 32, 34, 40, 46, 128
NT_DIMS = (((1,), (1,)), ((), ()))


def halves(a):
    hi = a.astype(BF16)
    return hi, (a - hi.astype(F32)).astype(BF16)


def rows4(re, im):
    rh = re.astype(BF16).astype(F32)
    ih = im.astype(BF16).astype(F32)
    return jnp.concatenate([rh, ih, re - rh, im - ih], axis=0).astype(BF16)


def nt(a, b):
    return lax.dot_general(a, b, NT_DIMS, preferred_element_type=F32)


def in_two(matrix, start, stop, right):
    half = TD // 2
    parts = [nt(matrix[at * TILE : (at + half) * TILE, start:stop], right) for at in (0, half)]
    return [parts[t // half][t % half * TILE : (t % half + 1) * TILE] for t in range(TD)]


def own_columns(blocks):
    lane = lax.broadcasted_iota(jnp.int32, blocks[0].shape, 1) % TD
    totals = [jnp.zeros_like(blocks[0])] * 2
    for t in range(TD):
        totals[t // (TD // 2)] = jnp.where(lane == t, blocks[t], totals[t // (TD // 2)])
    return totals[0] + totals[1]


def fold(columns):
    rows = columns.T
    re, im = rows[0:8], rows[8:16]
    for at in range(16, rows.shape[0], 16):
        re = re + rows[at : at + 8]
        im = im + rows[at + 8 : at + 16]
    return re, im


def gram(top, bottom):
    th, tl = halves(top)
    bh, bl = halves(bottom)
    return nt(jnp.concatenate([th, tl, th, tl], axis=1), jnp.concatenate([bh, bh, bl, bl], axis=1))


def solve(entry):
    def g_re(a, b):
        return entry(2 * b, UROW + 2 * a) + entry(2 * b + 1, UROW + 2 * a + 1)

    def g_im(a, b):
        return entry(2 * b + 1, UROW + 2 * a) - entry(2 * b, UROW + 2 * a + 1)

    real, imag = {}, {}
    for a in range(ITERS):
        for b in range(a + 1):
            real[a, b] = real[b, a] = g_re(a, b)
            if a != b:
                imag[a, b] = g_im(a, b)
                imag[b, a] = -imag[a, b]
            else:
                imag[a, a] = jnp.zeros_like(real[a, a])
    order = 2 * ITERS
    matrix = {}
    for i in range(order):
        for j in range(i + 1):
            a, b = i % ITERS, j % ITERS
            matrix[i, j] = real[a, b] if (i < ITERS) == (j < ITERS) else imag[a, b]
    vector = [g_re(a, ITERS) for a in range(ITERS)] + [g_im(a, ITERS) for a in range(ITERS)]
    lower, inverse = {}, {}
    for i in range(order):
        for j in range(i + 1):
            value = matrix[i, j]
            for k in range(j):
                value = value - lower[i, k] * lower[j, k]
            if i == j:
                inverse[i] = 1.0 / jnp.sqrt(value)
            else:
                lower[i, j] = value * inverse[j]
    forward = []
    for i in range(order):
        value = vector[i]
        for k in range(i):
            value = value - lower[i, k] * forward[k]
        forward.append(value * inverse[i])
    result = [None] * order
    for i in reversed(range(order)):
        value = forward[i]
        for k in range(i + 1, order):
            value = value - lower[k, i] * result[k]
        result[i] = value * inverse[i]
    return result[:ITERS], result[ITERS:]


def kernel(
    sizes,
    pattern,
    c_rows,
    c_side,
    c_count,
    shifts,
    weights,
    compact,
    fresh,
    mass,
    basis,
    k_hbm,
    p_hbm,
    c_hbm,
    made,
    listed,
    k_raw,
    p_raw,
    c_raw,
    k_two,
    p_two,
    c_two,
    stack,
    coef_table,
    weight_rows,
    right_coef,
    basis_gram,
    picked,
    tiles0,
    tiles1,
    tiles2,
    halo,
    sums,
    basis_sums,
    slot_masks,
    load_sem,
    tile_send,
    tile_recv,
    halo_send,
    halo_recv,
    sum_send,
    sum_recv,
    basis_send,
    basis_recv,
):
    ny, nz, nc, ns = sizes
    steps = weights.shape[0]
    total_rows = float(ny * nz * nc * ns * TD * TILE)
    n_dom = ny * nz * nc
    dom, sub = lax.axis_index("dom"), lax.axis_index("sub")
    core, chip_z, chip_y = dom % nc, (dom // nc) % nz, dom // (nc * nz)

    def at(y, z, c):
        return (y * nz + z) * nc + c

    def along(stage, d):
        if stage == 0:
            return (dom, (sub + d) % ns)
        if stage == 1:
            return (at((chip_y + d) % ny, chip_z, core), sub)
        return (at(chip_y, (chip_z + d // nc) % nz, (core + d) % nc), sub)

    extents = (ns, ny, nz * nc)
    places = (sub, chip_y, chip_z * nc + core)
    stages = len(extents)

    def order(stage):
        chips, cores = extents[stage] // (nc if stage == 2 else 1), nc if stage == 2 else 1
        return sorted(range(1, extents[stage]), key=lambda d: -min(d // cores, chips - d // cores))

    def send_sum(store, prefix, send_sem, recv_sem, stage):
        mine = store.at[(*prefix, stage, places[stage])]
        for d in order(stage):
            pltpu.make_async_remote_copy(
                src_ref=mine,
                dst_ref=mine,
                send_sem=send_sem.at[(*prefix, stage)],
                recv_sem=recv_sem.at[(*prefix, stage)],
                device_id=along(stage, d),
                device_id_type=MESH,
            ).start()

    def wait_for(ref, sem):
        pltpu.make_async_copy(ref, ref, sem).wait()

    def finish_sum(store, prefix, send_sem, recv_sem, stage):
        others = store.at[(*prefix, stage, pl.ds(0, extents[stage] - 1))]
        wait_for(others, recv_sem.at[(*prefix, stage)])
        total = store[(*prefix, stage, 0)]
        for other in range(1, extents[stage]):
            total = total + store[(*prefix, stage, other)]
        wait_for(others, send_sem.at[(*prefix, stage)])
        return total
    lower_dom, upper_dom = ((dom + n_dom - 1) % n_dom, sub), ((dom + 1) % n_dom, sub)

    loads = [
        pltpu.make_async_copy(basis.at[0], stack.at[pl.ds(0, NB)], load_sem.at[0]),
        pltpu.make_async_copy(basis.at[1], stack.at[pl.ds(NB, NB)], load_sem.at[1]),
        pltpu.make_async_copy(p_hbm, p_raw, load_sem.at[2]),
        pltpu.make_async_copy(k_hbm, k_raw, load_sem.at[3]),
        pltpu.make_async_copy(c_hbm, c_raw, load_sem.at[4]),
    ]
    for load in loads:
        load.start()

    barrier = pltpu.get_barrier_semaphore()
    greeted = 0
    for stage in range(stages):
        for d in range(1, extents[stage]):
            pl.semaphore_signal(barrier, inc=1, device_id=along(stage, d), device_id_type=MESH)
            greeted += 1
    for who in (lower_dom, upper_dom):
        pl.semaphore_signal(barrier, inc=1, device_id=who, device_id_type=MESH)
        greeted += 1

    lane = lax.broadcasted_iota(jnp.int32, (8, TILE), 1)
    row = lax.broadcasted_iota(jnp.int32, (8, TILE), 0)
    lane2 = lax.broadcasted_iota(jnp.int32, (NB, TILE), 1)

    terms = weights.shape[2]
    coef_table[...] = jnp.zeros_like(coef_table)
    coef_table[0:NB, 0:terms] = compact[0]
    coef_table[0:NB, terms : 2 * terms] = compact[1]
    coef_table[NB : 2 * NB, 0:terms] = -compact[1]
    coef_table[NB : 2 * NB, terms : 2 * terms] = compact[0]
    weight_rows[...] = jnp.zeros_like(weight_rows)
    for k in range(steps):
        weight_rows[2 * k : 2 * k + 1, 0:terms] = weights[k, 0:1, :]
        weight_rows[2 * k : 2 * k + 1, terms : 2 * terms] = -weights[k, 1:2, :]
        weight_rows[2 * k + 1 : 2 * k + 2, 0:terms] = weights[k, 1:2, :]
        weight_rows[2 * k + 1 : 2 * k + 2, terms : 2 * terms] = weights[k, 0:1, :]
    mixed_rows = lax.dot_general(
        weight_rows[...], coef_table[...], NT_DIMS, precision=HIGH, preferred_element_type=F32
    )
    for k in range(steps):
        wr, wi = weights[k, 0:1, :], weights[k, 1:2, :]
        fr, fi = fresh[0:1, :], fresh[1:2, :]
        gr = jnp.sum(wr * fr - wi * fi, axis=1, keepdims=True)
        gi = jnp.sum(wr * fi + wi * fr, axis=1, keepdims=True)
        line = lane[0:1]
        first = mixed_rows[2 * k : 2 * k + 1]
        second = mixed_rows[2 * k + 1 : 2 * k + 2]
        first = jnp.where(line == PREV, gr, jnp.where(line == PREV + 1, -gi, first))
        second = jnp.where(line == PREV, gi, jnp.where(line == PREV + 1, gr, second))
        right_coef[k] = jnp.zeros((8, TILE), F32)
        right_coef[k, 0:1, :] = first
        right_coef[k, 1:2, :] = second

    stack[pl.ds(PREV, 16), :] = jnp.zeros((16, TD * TILE), F32)
    loads[0].wait()
    loads[1].wait()

    loads[2].wait()

    @pl.loop(0, TD)
    def _(t):
        for c in range(2):
            hi, lo = halves(p_raw[t, c])
            p_two[pl.ds(t * TILE, TILE), (2 * c) * TILE : (2 * c + 1) * TILE] = hi
            p_two[pl.ds(t * TILE, TILE), (2 * c + 1) * TILE : (2 * c + 2) * TILE] = lo

    gathered = (tiles0, tiles1, tiles2)

    def late_start():
        slot_lane = lax.broadcasted_iota(jnp.int32, (1, 64), 1)
        for j in range(TD):
            live = j < c_count[0]
            present = jnp.where(c_side[j] == 0, (dom > 0).astype(jnp.int32), (dom < n_dom - 1).astype(jnp.int32))
            on = jnp.where(live, present, 0)
            hit = (slot_lane // 32 == c_side[j]) & (slot_lane % TD == c_rows[j])
            slot_masks[j : j + 1, :] = jnp.where(hit, on, 0).astype(F32)

        stack[pl.ds(PREV + 16, XROWS - PREV - 16), :] = jnp.zeros((XROWS - PREV - 16, TD * TILE), F32)
        wide = gram(stack[0 : 2 * NB, :], stack[0:XROWS, :])
        basis_gram[...] = jnp.zeros_like(basis_gram)
        basis_gram[:, 0:XROWS] = wide
        upper, under = basis_gram[0:NB, :], basis_gram[NB : 2 * NB, :]
        mixed = upper + jnp.where(lane2 < NB, pltpu.roll(under, TILE - NB, 1), -pltpu.roll(under, NB, 1))
        mixed = jnp.where(lane2 < 2 * NB, mixed, 0.0)
        basis_part = (
            mixed[0:4] + pltpu.roll(mixed[4:8], 32, 1) + pltpu.roll(mixed[8:12], 64, 1) + pltpu.roll(mixed[12:16], 96, 1)
        )
        basis_sums[0, places[0]] = basis_part

        send_sum(basis_sums, (), basis_send, basis_recv, 0)

    def split_rest():
        loads[3].wait()

        @pl.loop(0, TD)
        def _(t):
            for q in range(3):
                hi, lo = halves(k_raw[t, q])
                k_two[pl.ds(t * TILE, TILE), (2 * q) * TILE : (2 * q + 1) * TILE] = hi
                k_two[pl.ds(t * TILE, TILE), (2 * q + 1) * TILE : (2 * q + 2) * TILE] = lo

        loads[4].wait()

        @pl.loop(0, TD)
        def _(t):
            hi, lo = halves(c_raw[t])
            c_two[pl.ds(t * TILE, TILE), 0:TILE] = hi
            c_two[pl.ds(t * TILE, TILE), TILE : 2 * TILE] = lo

    def to_stack(at_row, re, im):
        for t in range(TD):
            stack[at_row : at_row + 1, t * TILE : (t + 1) * TILE] = re[t : t + 1]
            stack[at_row + 1 : at_row + 2, t * TILE : (t + 1) * TILE] = im[t : t + 1]

    def one_step(step):
        right = jnp.dot(
            right_coef[step][:, 0:UROW], stack[0:UROW, :], precision=HIGH, preferred_element_type=F32
        )
        stack[RIGHT : RIGHT + 2, :] = right[0:2]
        t_re = jnp.concatenate([right[0:1, t * TILE : (t + 1) * TILE] for t in range(TD)], axis=0)
        t_im = jnp.concatenate([right[1:2, t * TILE : (t + 1) * TILE] for t in range(TD)], axis=0)
        shift_re, shift_im = shifts[step, 0], shifts[step, 1]
        for it in range(ITERS):
            tiles = gathered[it]
            plain, turned = rows4(t_re, t_im), rows4(-t_im, t_re)
            blocks = in_two(p_two, 0, 4 * TILE, jnp.concatenate([plain, plain, turned, turned], axis=1))
            z_re, z_im = fold(own_columns(blocks))
            tiles[sub, 0] = z_re
            tiles[sub, 1] = z_im
            if it == 0:

                @pl.when(step == 0)
                def _():
                    pl.semaphore_wait(barrier, greeted)

            turn = step * ITERS + it
            for side, who in ((1, lower_dom), (0, upper_dom)):
                pltpu.make_async_remote_copy(
                    src_ref=tiles.at[sub],
                    dst_ref=halo.at[turn, side],
                    send_sem=halo_send.at[turn],
                    recv_sem=halo_recv.at[turn],
                    device_id=who,
                    device_id_type=MESH,
                ).start()
            for d in order(0):
                pltpu.make_async_remote_copy(
                    src_ref=tiles.at[sub],
                    dst_ref=tiles.at[sub],
                    send_sem=tile_send.at[turn],
                    recv_sem=tile_recv.at[turn],
                    device_id=along(0, d),
                    device_id_type=MESH,
                ).start()
            if it == 0:

                @pl.when(step == 0)
                def _():
                    split_rest()
                    late_start()

            else:

                @pl.when(step == 0)
                def _():
                    so_far = finish_sum(basis_sums, (), basis_send, basis_recv, it - 1)
                    basis_sums[it, places[it]] = so_far
                    send_sum(basis_sums, (), basis_send, basis_recv, it)

            to_stack(ZROW + 2 * it, z_re, z_im)
            own = rows4(z_re, z_im)
            blocks = in_two(k_two, 0, 2 * TILE, jnp.concatenate([own, own], axis=1))
            u_re, u_im = fold(own_columns(blocks))
            moved_re, moved_im = mass[...] * z_re, mass[...] * z_im
            u_re = u_re - (shift_re * moved_re - shift_im * moved_im)
            u_im = u_im - (shift_re * moved_im + shift_im * moved_re)

            if it == ITERS - 1:
                both = gram(stack[PREV : RIGHT + 2, :], stack[0:XROWS, :])
                packed = jnp.where(lane < UROW, both[0:8], jnp.where(lane < RIGHT + 2, both[8:16], 0.0))

            wait_for(halo.at[turn], halo_recv.at[turn])
            sides = []
            for side, tile in ((0, TD - 1), (1, 0)):
                re = jnp.broadcast_to(halo[turn, side, 0, tile : tile + 1, :], (8, TILE))
                im = jnp.broadcast_to(halo[turn, side, 1, tile : tile + 1, :], (8, TILE))
                sides.append(rows4(re, im))
            rims = jnp.concatenate(sides, axis=0)
            blocks = in_two(c_two, 0, 2 * TILE, jnp.concatenate([rims, rims], axis=1))
            columns = jnp.zeros((TILE, 64), F32)
            for j in range(TD):
                columns = columns + slot_masks[j : j + 1, :] * blocks[j]
            c_re, c_im = fold(columns)
            u_re, u_im = u_re + c_re, u_im + c_im

            wait_for(tiles.at[pl.ds(0, ns - 1)], tile_recv.at[turn])
            for q in range(2):
                for t in range(TD):
                    source = pattern[q, t]
                    for c in range(2):
                        picked[q, c, t : t + 1, :] = tiles[source // TD, c, pl.ds(source % TD, 1), :]
            first = rows4(picked[0, 0], picked[0, 1])
            second = rows4(picked[1, 0], picked[1, 1])
            blocks = in_two(k_two, 2 * TILE, 6 * TILE, jnp.concatenate([first, first, second, second], axis=1))
            k_re, k_im = fold(own_columns(blocks))
            u_re, u_im = u_re + k_re, u_im + k_im
            to_stack(UROW + 2 * it, u_re, u_im)
            t_re, t_im = u_re - t_re, u_im - t_im
            if it == ITERS - 1:
                with_u_re = jnp.zeros((8, TILE), F32)
                with_u_im = jnp.zeros((8, TILE), F32)
                for t in range(TD):
                    block = stack[UROW : RIGHT + 2, t * TILE : (t + 1) * TILE]
                    with_u_re = with_u_re + block * u_re[t : t + 1]
                    with_u_im = with_u_im + block * u_im[t : t + 1]
                with_u_re = jnp.sum(with_u_re, axis=1, keepdims=True)
                with_u_im = jnp.sum(with_u_im, axis=1, keepdims=True)
                last = UROW + 2 * it
                packed = jnp.where(lane == last, with_u_re, jnp.where(lane == last + 1, with_u_im, packed))
            wait_for(halo.at[turn], halo_send.at[turn])
            wait_for(tiles.at[pl.ds(0, ns - 1)], tile_send.at[turn])

        part = packed[0:4] + pltpu.roll(packed[4:8], 64, 1)
        for stage in range(stages):
            sums[step, stage, places[stage]] = part
            send_sum(sums, (step,), sum_send, sum_recv, stage)
            part = finish_sum(sums, (step,), sum_send, sum_recv, stage)
        reduced = jnp.concatenate([part, pltpu.roll(part, 64, 1)], axis=0)

        def entry(i, j):
            return jnp.broadcast_to(reduced[i : i + 1, j : j + 1], (8, TILE))

        def line_of(i):
            return jnp.broadcast_to(reduced[i : i + 1, :], (8, TILE))

        y_re, y_im = solve(entry)
        with_re = jnp.zeros((8, TILE), F32)
        with_im = jnp.zeros((8, TILE), F32)
        sol_re = jnp.zeros((8, TILE), F32)
        sol_im = jnp.zeros((8, TILE), F32)
        for j in range(ITERS):
            a, b = line_of(2 + 2 * j), line_of(3 + 2 * j)
            with_re = with_re + (y_re[j] * a - y_im[j] * b)
            with_im = with_im + (y_re[j] * b + y_im[j] * a)
            here, after = lane == ZROW + 2 * j, lane == ZROW + 2 * j + 1
            sol_re = jnp.where(here, y_re[j], jnp.where(after, -y_im[j], sol_re))
            sol_im = jnp.where(here, y_im[j], jnp.where(after, y_re[j], sol_im))

        def back(a, n):
            return pltpu.roll(a, TILE - n, 1)

        on_basis, on_prev = lane < NB, lane == PREV
        h_re = jnp.where(
            on_basis, with_re + back(with_im, NB), jnp.where(on_prev, with_re + back(with_im, 1), 0.0)
        )
        h_im = jnp.where(
            on_basis, with_im - back(with_re, NB), jnp.where(on_prev, with_im - back(with_re, 1), 0.0)
        )
        h_re, h_im = h_re / total_rows, h_im / total_rows
        on_imag, on_prev_imag = (lane >= NB) & (lane < 2 * NB), lane == PREV + 1
        e_re = h_re - jnp.where(
            on_imag, pltpu.roll(h_im, NB, 1), jnp.where(on_prev_imag, pltpu.roll(h_im, 1, 1), 0.0)
        )
        e_im = h_im + jnp.where(
            on_imag, pltpu.roll(h_re, NB, 1), jnp.where(on_prev_imag, pltpu.roll(h_re, 1, 1), 0.0)
        )

        @pl.when(step == 0)
        def _():
            whole = finish_sum(basis_sums, (), basis_send, basis_recv, stages - 1)
            blocks = [whole] + [pltpu.roll(whole, TILE - shift, 1) for shift in (32, 64, 96)]
            basis_gram[0:NB, :] = jnp.where(lane2 < 2 * NB, jnp.concatenate(blocks, axis=0), 0.0)

        pair = jnp.where(row == 0, e_re, jnp.where(row == 1, e_im, 0.0))
        turned = jnp.dot(pair[:, 0:NB], basis_gram[0:NB, :], precision=HIGH, preferred_element_type=F32)
        p_re = jnp.broadcast_to(h_re[0:1, PREV : PREV + 1], (8, TILE))
        p_im = jnp.broadcast_to(h_im[0:1, PREV : PREV + 1], (8, TILE))
        prev_re, prev_im = line_of(0), line_of(1)
        v_re, v_im = p_re * prev_re - p_im * prev_im, p_im * prev_re + p_re * prev_im
        share = jnp.where(lane < PREV, 2.0, jnp.where(lane < PREV + 2, 1.0, 0.0))
        first_row = (
            sol_re * with_re
            + sol_im * with_im
            - 2.0 * total_rows * (h_re * h_re + h_im * h_im)
            + share * (v_re * e_re + v_im * e_im)
        )
        first_row = jnp.where(lane < UROW, first_row, 0.0)
        each = turned * pair + jnp.where(row == 0, first_row, 0.0)
        squares = jnp.sum(jnp.sum(each, axis=0, keepdims=True), axis=1, keepdims=True)
        squares = jnp.broadcast_to(squares, (8, TILE))
        norm = jnp.sqrt(jnp.maximum(squares, 0.0) / total_rows + EPSILON)

        coef = jnp.where(row == 0, sol_re - e_re, jnp.where(row == 1, sol_im - e_im, 0.0)) / norm
        latest = jnp.dot(coef[:, 0:UROW], stack[0:UROW, :], precision=HIGH, preferred_element_type=F32)
        made[step] = latest[0:2]
        stack[PREV : PREV + 2, :] = latest[0:2]
        top = jnp.where(on_basis, h_re, jnp.where(lane == NB, back(h_re, NB), norm))
        low = jnp.where(on_basis, h_im, jnp.where(lane == NB, back(h_im, NB), 0.0))
        listed[step, 0:1, :] = top[0:1, 0 : NB + 2]
        listed[step, 1:2, :] = low[0:1, 0 : NB + 2]

    @pl.loop(0, steps)
    def _(step):
        one_step(step)


def hand_over(made, listed, made_out, listed_out):
    made_out[...] = made[...]
    listed_out[...] = listed[...]


def solution(mesh, y_chips=None):
    ns, n_dom = mesh.shape["sub"], mesh.shape["dom"]
    nz = Z_CHIPS if y_chips is None else n_dom // CORES // y_chips
    sizes = (n_dom // (CORES * nz), nz, CORES, ns)
    most = max(ns, sizes[0], nz * CORES)

    def local(basis, compact, weights, fresh, shifts, k_tiles, pattern, mass, precond, c_tiles, c_rows, c_side, c_count):
        smem = pl.BlockSpec(memory_space=pltpu.SMEM)
        vmem = pl.BlockSpec(memory_space=pltpu.VMEM)
        anywhere = pl.BlockSpec(memory_space=pl.ANY)
        steps = weights.shape[0]
        rows = TD * TILE
        made, listed = pl.pallas_call(
            functools.partial(kernel, sizes),
            out_shape=(
                jax.ShapeDtypeStruct((steps, 2, rows), F32),
                jax.ShapeDtypeStruct((steps, 2, NB + 2), F32),
            ),
            in_specs=[smem] * 5 + [vmem] * 4 + [anywhere] * 4,
            out_specs=(vmem, vmem),
            scratch_shapes=[
                pltpu.VMEM((TD, 3, TILE, TILE), F32),
                pltpu.VMEM((TD, 2, TILE, TILE), F32),
                pltpu.VMEM((TD, TILE, TILE), F32),
                pltpu.VMEM((rows, 6 * TILE), BF16),
                pltpu.VMEM((rows, 4 * TILE), BF16),
                pltpu.VMEM((rows, 2 * TILE), BF16),
                pltpu.VMEM((XROWS, rows), F32),
                pltpu.VMEM((TILE, TILE), F32),
                pltpu.VMEM((8, TILE), F32),
                pltpu.VMEM((steps, 8, TILE), F32),
                pltpu.VMEM((2 * NB, TILE), F32),
                pltpu.VMEM((2, 2, TD, TILE), F32),
                pltpu.VMEM((ns, 2, TD, TILE), F32),
                pltpu.VMEM((ns, 2, TD, TILE), F32),
                pltpu.VMEM((ns, 2, TD, TILE), F32),
                pltpu.VMEM((steps * ITERS, 2, 2, TD, TILE), F32),
                pltpu.VMEM((steps, 3, most, 4, TILE), F32),
                pltpu.VMEM((3, most, 4, TILE), F32),
                pltpu.VMEM((TD, 64), F32),
                pltpu.SemaphoreType.DMA((5,)),
                pltpu.SemaphoreType.DMA((steps * ITERS,)),
                pltpu.SemaphoreType.DMA((steps * ITERS,)),
                pltpu.SemaphoreType.DMA((steps * ITERS,)),
                pltpu.SemaphoreType.DMA((steps * ITERS,)),
                pltpu.SemaphoreType.DMA((steps, 3)),
                pltpu.SemaphoreType.DMA((steps, 3)),
                pltpu.SemaphoreType.DMA((3,)),
                pltpu.SemaphoreType.DMA((3,)),
            ],
            compiler_params=pltpu.CompilerParams(collective_id=0, has_side_effects=True),
        )(
            pattern.T,
            c_rows,
            c_side,
            c_count,
            shifts,
            weights,
            jnp.swapaxes(compact, 1, 2),
            fresh,
            mass.reshape(TD, TILE),
            basis,
            k_tiles,
            precond,
            c_tiles,
        )
        return pl.pallas_call(
            hand_over,
            out_shape=(
                jax.ShapeDtypeStruct((steps, 2, rows), F32),
                jax.ShapeDtypeStruct((steps, 2, NB + 2), F32),
            ),
            in_specs=[vmem] * 2,
            out_specs=(vmem, vmem),
        )(made, listed)

    both = ("dom", "sub")
    placed = (
        P(None, None, both),
        P(),
        P(),
        P(),
        P(),
        P(both, None, None, None),
        P(both, None),
        P(both),
        P(both, None, None, None),
        P(both, None, None),
        P(both),
        P(both),
        P(both),
    )
    return jax.shard_map(
        local, mesh=mesh, in_specs=placed, out_specs=(P(None, None, both), P()), check_vma=False
    )
```

```python
import functools

import jax
import jax.numpy as jnp
from jax import lax
from jax.experimental import pallas as pl
from jax.experimental.pallas import tpu as pltpu
from jax.sharding import PartitionSpec as P

MESH = pl.DeviceIdType.MESH
HIGH = lax.Precision.HIGHEST
F32 = jnp.float32
BF16 = jnp.bfloat16
EPSILON = 1e-06

ITERS = 3
TD = 8
TILE = 128
NB = 16
CORES = 2
Z_CHIPS = 8

PREV, ZROW, UROW, RIGHT, XROWS = 32, 34, 40, 46, 128
NT_DIMS = (((1,), (1,)), ((), ()))


def halves(a):
    hi = a.astype(BF16)
    return hi, (a - hi.astype(F32)).astype(BF16)


def rows4(re, im):
    rh = re.astype(BF16).astype(F32)
    ih = im.astype(BF16).astype(F32)
    return jnp.concatenate([rh, ih, re - rh, im - ih], axis=0).astype(BF16)


def nt(a, b):
    return lax.dot_general(a, b, NT_DIMS, preferred_element_type=F32)


def in_two(matrix, start, stop, right):
    half = TD // 2
    parts = [nt(matrix[at * TILE : (at + half) * TILE, start:stop], right) for at in (0, half)]
    return [parts[t // half][t % half * TILE : (t % half + 1) * TILE] for t in range(TD)]


def own_columns(blocks):
    lane = lax.broadcasted_iota(jnp.int32, blocks[0].shape, 1) % TD
    totals = [jnp.zeros_like(blocks[0])] * 2
    for t in range(TD):
        totals[t // (TD // 2)] = jnp.where(lane == t, blocks[t], totals[t // (TD // 2)])
    return totals[0] + totals[1]


def fold(columns):
    rows = columns.T
    re, im = rows[0:8], rows[8:16]
    for at in range(16, rows.shape[0], 16):
        re = re + rows[at : at + 8]
        im = im + rows[at + 8 : at + 16]
    return re, im


def gram(top, bottom):
    th, tl = halves(top)
    bh, bl = halves(bottom)
    return nt(jnp.concatenate([th, tl, th, tl], axis=1), jnp.concatenate([bh, bh, bl, bl], axis=1))


def solve(entry):
    def g_re(a, b):
        return entry(2 * b, UROW + 2 * a) + entry(2 * b + 1, UROW + 2 * a + 1)

    def g_im(a, b):
        return entry(2 * b + 1, UROW + 2 * a) - entry(2 * b, UROW + 2 * a + 1)

    real, imag = {}, {}
    for a in range(ITERS):
        for b in range(a + 1):
            real[a, b] = real[b, a] = g_re(a, b)
            if a != b:
                imag[a, b] = g_im(a, b)
                imag[b, a] = -imag[a, b]
            else:
                imag[a, a] = jnp.zeros_like(real[a, a])
    order = 2 * ITERS
    matrix = {}
    for i in range(order):
        for j in range(i + 1):
            a, b = i % ITERS, j % ITERS
            matrix[i, j] = real[a, b] if (i < ITERS) == (j < ITERS) else imag[a, b]
    vector = [g_re(a, ITERS) for a in range(ITERS)] + [g_im(a, ITERS) for a in range(ITERS)]
    lower, inverse = {}, {}
    for i in range(order):
        for j in range(i + 1):
            value = matrix[i, j]
            for k in range(j):
                value = value - lower[i, k] * lower[j, k]
            if i == j:
                inverse[i] = 1.0 / jnp.sqrt(value)
            else:
                lower[i, j] = value * inverse[j]
    forward = []
    for i in range(order):
        value = vector[i]
        for k in range(i):
            value = value - lower[i, k] * forward[k]
        forward.append(value * inverse[i])
    result = [None] * order
    for i in reversed(range(order)):
        value = forward[i]
        for k in range(i + 1, order):
            value = value - lower[k, i] * result[k]
        result[i] = value * inverse[i]
    return result[:ITERS], result[ITERS:]


def kernel(
    sizes,
    pattern_hbm,
    c_rows_hbm,
    c_side_hbm,
    c_count,
    shifts_hbm,
    weights_hbm,
    compact_hbm,
    fresh_hbm,
    mass_hbm,
    basis,
    k_hbm,
    p_hbm,
    c_hbm,
    made,
    listed,
    k_raw,
    p_raw,
    c_raw,
    k_two,
    p_two,
    c_two,
    stack,
    coef_table,
    weight_rows,
    right_coef,
    basis_gram,
    picked,
    tiles0,
    tiles1,
    tiles2,
    halo,
    sums,
    basis_sums,
    slot_masks,
    pattern,
    c_rows,
    c_side,
    shifts,
    weights,
    compact,
    fresh,
    mass,
    load_sem,
    tile_send,
    tile_recv,
    halo_send,
    halo_recv,
    sum_send,
    sum_recv,
    basis_send,
    basis_recv,
):
    ny, nz, nc, ns = sizes
    steps = weights.shape[0]
    total_rows = float(ny * nz * nc * ns * TD * TILE)
    n_dom = ny * nz * nc
    dom, sub = lax.axis_index("dom"), lax.axis_index("sub")
    core, chip_z, chip_y = dom % nc, (dom // nc) % nz, dom // (nc * nz)

    def at(y, z, c):
        return (y * nz + z) * nc + c

    def along(stage, d):
        if stage == 0:
            return (dom, (sub + d) % ns)
        if stage == 1:
            return (at((chip_y + d) % ny, chip_z, core), sub)
        return (at(chip_y, (chip_z + d // nc) % nz, (core + d) % nc), sub)

    extents = (ns, ny, nz * nc)
    places = (sub, chip_y, chip_z * nc + core)
    stages = len(extents)

    def order(stage):
        chips, cores = extents[stage] // (nc if stage == 2 else 1), nc if stage == 2 else 1
        return sorted(range(1, extents[stage]), key=lambda d: -min(d // cores, chips - d // cores))

    def send_sum(store, prefix, send_sem, recv_sem, stage):
        mine = store.at[(*prefix, stage, places[stage])]
        for d in order(stage):
            pltpu.make_async_remote_copy(
                src_ref=mine,
                dst_ref=mine,
                send_sem=send_sem.at[(*prefix, stage)],
                recv_sem=recv_sem.at[(*prefix, stage)],
                device_id=along(stage, d),
                device_id_type=MESH,
            ).start()

    def wait_for(ref, sem):
        pltpu.make_async_copy(ref, ref, sem).wait()

    def finish_sum(store, prefix, send_sem, recv_sem, stage):
        others = store.at[(*prefix, stage, pl.ds(0, extents[stage] - 1))]
        wait_for(others, recv_sem.at[(*prefix, stage)])
        total = store[(*prefix, stage, 0)]
        for other in range(1, extents[stage]):
            total = total + store[(*prefix, stage, other)]
        wait_for(others, send_sem.at[(*prefix, stage)])
        return total
    lower_dom, upper_dom = ((dom + n_dom - 1) % n_dom, sub), ((dom + 1) % n_dom, sub)

    pairs = (
        (weights_hbm, weights),
        (compact_hbm, compact),
        (fresh_hbm, fresh),
        (basis.at[0], stack.at[pl.ds(0, NB)]),
        (basis.at[1], stack.at[pl.ds(NB, NB)]),
        (p_hbm, p_raw),
        (shifts_hbm, shifts),
        (mass_hbm, mass),
        (pattern_hbm, pattern),
        (c_rows_hbm, c_rows),
        (c_side_hbm, c_side),
        (k_hbm, k_raw),
        (c_hbm, c_raw),
    )
    loads = [pltpu.make_async_copy(source, target, load_sem.at[n]) for n, (source, target) in enumerate(pairs)]
    for load in loads:
        load.start()

    barrier = pltpu.get_barrier_semaphore()
    greeted = 0
    for stage in range(stages):
        for d in order(stage):
            pl.semaphore_signal(barrier, inc=1, device_id=along(stage, d), device_id_type=MESH)
            greeted += 1
    for who in (lower_dom, upper_dom):
        pl.semaphore_signal(barrier, inc=1, device_id=who, device_id_type=MESH)
        greeted += 1

    lane = lax.broadcasted_iota(jnp.int32, (8, TILE), 1)
    row = lax.broadcasted_iota(jnp.int32, (8, TILE), 0)
    lane2 = lax.broadcasted_iota(jnp.int32, (NB, TILE), 1)

    for load in loads[0:3]:
        load.wait()

    terms = weights.shape[2]
    coef_table[...] = jnp.zeros_like(coef_table)
    coef_table[0:NB, 0:terms] = compact[0]
    coef_table[0:NB, terms : 2 * terms] = compact[1]
    coef_table[NB : 2 * NB, 0:terms] = -compact[1]
    coef_table[NB : 2 * NB, terms : 2 * terms] = compact[0]
    weight_rows[...] = jnp.zeros_like(weight_rows)
    for k in range(steps):
        weight_rows[2 * k : 2 * k + 1, 0:terms] = weights[k, 0:1, :]
        weight_rows[2 * k : 2 * k + 1, terms : 2 * terms] = -weights[k, 1:2, :]
        weight_rows[2 * k + 1 : 2 * k + 2, 0:terms] = weights[k, 1:2, :]
        weight_rows[2 * k + 1 : 2 * k + 2, terms : 2 * terms] = weights[k, 0:1, :]
    mixed_rows = lax.dot_general(
        weight_rows[...], coef_table[...], NT_DIMS, precision=HIGH, preferred_element_type=F32
    )
    for k in range(steps):
        wr, wi = weights[k, 0:1, :], weights[k, 1:2, :]
        fr, fi = fresh[0:1, :], fresh[1:2, :]
        gr = jnp.sum(wr * fr - wi * fi, axis=1, keepdims=True)
        gi = jnp.sum(wr * fi + wi * fr, axis=1, keepdims=True)
        line = lane[0:1]
        first = mixed_rows[2 * k : 2 * k + 1]
        second = mixed_rows[2 * k + 1 : 2 * k + 2]
        first = jnp.where(line == PREV, gr, jnp.where(line == PREV + 1, -gi, first))
        second = jnp.where(line == PREV, gi, jnp.where(line == PREV + 1, gr, second))
        right_coef[k] = jnp.zeros((8, TILE), F32)
        right_coef[k, 0:1, :] = first
        right_coef[k, 1:2, :] = second

    stack[pl.ds(PREV, 16), :] = jnp.zeros((16, TD * TILE), F32)
    for load in loads[3:6]:
        load.wait()

    @pl.loop(0, TD)
    def _(t):
        for c in range(2):
            hi, lo = halves(p_raw[t, c])
            p_two[pl.ds(t * TILE, TILE), (2 * c) * TILE : (2 * c + 1) * TILE] = hi
            p_two[pl.ds(t * TILE, TILE), (2 * c + 1) * TILE : (2 * c + 2) * TILE] = lo

    for load in loads[6:11]:
        load.wait()
    gathered = (tiles0, tiles1, tiles2)

    def late_start():
        slot_lane = lax.broadcasted_iota(jnp.int32, (1, 64), 1)
        for j in range(TD):
            live = j < c_count[0]
            present = jnp.where(c_side[j] == 0, (dom > 0).astype(jnp.int32), (dom < n_dom - 1).astype(jnp.int32))
            on = jnp.where(live, present, 0)
            hit = (slot_lane // 32 == c_side[j]) & (slot_lane % TD == c_rows[j])
            slot_masks[j : j + 1, :] = jnp.where(hit, on, 0).astype(F32)

        stack[pl.ds(PREV + 16, XROWS - PREV - 16), :] = jnp.zeros((XROWS - PREV - 16, TD * TILE), F32)
        wide = gram(stack[0 : 2 * NB, :], stack[0:XROWS, :])
        basis_gram[...] = jnp.zeros_like(basis_gram)
        basis_gram[:, 0:XROWS] = wide
        upper, under = basis_gram[0:NB, :], basis_gram[NB : 2 * NB, :]
        mixed = upper + jnp.where(lane2 < NB, pltpu.roll(under, TILE - NB, 1), -pltpu.roll(under, NB, 1))
        mixed = jnp.where(lane2 < 2 * NB, mixed, 0.0)
        basis_part = (
            mixed[0:4] + pltpu.roll(mixed[4:8], 32, 1) + pltpu.roll(mixed[8:12], 64, 1) + pltpu.roll(mixed[12:16], 96, 1)
        )
        basis_sums[0, places[0]] = basis_part

        send_sum(basis_sums, (), basis_send, basis_recv, 0)

    def split_rest():
        loads[11].wait()

        @pl.loop(0, TD)
        def _(t):
            for q in range(3):
                hi, lo = halves(k_raw[t, q])
                k_two[pl.ds(t * TILE, TILE), (2 * q) * TILE : (2 * q + 1) * TILE] = hi
                k_two[pl.ds(t * TILE, TILE), (2 * q + 1) * TILE : (2 * q + 2) * TILE] = lo

        loads[12].wait()

        @pl.loop(0, TD)
        def _(t):
            hi, lo = halves(c_raw[t])
            c_two[pl.ds(t * TILE, TILE), 0:TILE] = hi
            c_two[pl.ds(t * TILE, TILE), TILE : 2 * TILE] = lo

    def to_stack(at_row, re, im):
        for t in range(TD):
            stack[at_row : at_row + 1, t * TILE : (t + 1) * TILE] = re[t : t + 1]
            stack[at_row + 1 : at_row + 2, t * TILE : (t + 1) * TILE] = im[t : t + 1]

    def one_step(step):
        right = jnp.dot(
            right_coef[step][:, 0:UROW], stack[0:UROW, :], precision=HIGH, preferred_element_type=F32
        )
        stack[RIGHT : RIGHT + 2, :] = right[0:2]
        t_re = jnp.concatenate([right[0:1, t * TILE : (t + 1) * TILE] for t in range(TD)], axis=0)
        t_im = jnp.concatenate([right[1:2, t * TILE : (t + 1) * TILE] for t in range(TD)], axis=0)
        shift_re, shift_im = shifts[step, 0], shifts[step, 1]
        for it in range(ITERS):
            tiles = gathered[it]
            plain, turned = rows4(t_re, t_im), rows4(-t_im, t_re)
            blocks = in_two(p_two, 0, 4 * TILE, jnp.concatenate([plain, plain, turned, turned], axis=1))
            z_re, z_im = fold(own_columns(blocks))
            tiles[sub, 0] = z_re
            tiles[sub, 1] = z_im
            if it == 0:

                @pl.when(step == 0)
                def _():
                    pl.semaphore_wait(barrier, greeted)

            turn = step * ITERS + it
            for side, who in ((1, lower_dom), (0, upper_dom)):
                pltpu.make_async_remote_copy(
                    src_ref=tiles.at[sub],
                    dst_ref=halo.at[turn, side],
                    send_sem=halo_send.at[turn],
                    recv_sem=halo_recv.at[turn],
                    device_id=who,
                    device_id_type=MESH,
                ).start()
            for d in order(0):
                pltpu.make_async_remote_copy(
                    src_ref=tiles.at[sub],
                    dst_ref=tiles.at[sub],
                    send_sem=tile_send.at[turn],
                    recv_sem=tile_recv.at[turn],
                    device_id=along(0, d),
                    device_id_type=MESH,
                ).start()
            if it == 0:

                @pl.when(step == 0)
                def _():
                    split_rest()
                    late_start()

            else:

                @pl.when(step == 0)
                def _():
                    so_far = finish_sum(basis_sums, (), basis_send, basis_recv, it - 1)
                    basis_sums[it, places[it]] = so_far
                    send_sum(basis_sums, (), basis_send, basis_recv, it)

            to_stack(ZROW + 2 * it, z_re, z_im)
            own = rows4(z_re, z_im)
            blocks = in_two(k_two, 0, 2 * TILE, jnp.concatenate([own, own], axis=1))
            u_re, u_im = fold(own_columns(blocks))
            moved_re, moved_im = mass[...] * z_re, mass[...] * z_im
            u_re = u_re - (shift_re * moved_re - shift_im * moved_im)
            u_im = u_im - (shift_re * moved_im + shift_im * moved_re)

            if it == ITERS - 1:
                both = gram(stack[PREV : RIGHT + 2, :], stack[0:XROWS, :])
                packed = jnp.where(lane < UROW, both[0:8], jnp.where(lane < RIGHT + 2, both[8:16], 0.0))

            wait_for(halo.at[turn], halo_recv.at[turn])
            sides = []
            for side, tile in ((0, TD - 1), (1, 0)):
                re = jnp.broadcast_to(halo[turn, side, 0, tile : tile + 1, :], (8, TILE))
                im = jnp.broadcast_to(halo[turn, side, 1, tile : tile + 1, :], (8, TILE))
                sides.append(rows4(re, im))
            rims = jnp.concatenate(sides, axis=0)
            blocks = in_two(c_two, 0, 2 * TILE, jnp.concatenate([rims, rims], axis=1))
            columns = jnp.zeros((TILE, 64), F32)
            for j in range(TD):
                columns = columns + slot_masks[j : j + 1, :] * blocks[j]
            c_re, c_im = fold(columns)
            u_re, u_im = u_re + c_re, u_im + c_im

            wait_for(tiles.at[pl.ds(0, ns - 1)], tile_recv.at[turn])
            for q in range(2):
                for t in range(TD):
                    source = pattern[q, t]
                    for c in range(2):
                        picked[q, c, t : t + 1, :] = tiles[source // TD, c, pl.ds(source % TD, 1), :]
            first = rows4(picked[0, 0], picked[0, 1])
            second = rows4(picked[1, 0], picked[1, 1])
            blocks = in_two(k_two, 2 * TILE, 6 * TILE, jnp.concatenate([first, first, second, second], axis=1))
            k_re, k_im = fold(own_columns(blocks))
            u_re, u_im = u_re + k_re, u_im + k_im
            to_stack(UROW + 2 * it, u_re, u_im)
            t_re, t_im = u_re - t_re, u_im - t_im
            if it == ITERS - 1:
                with_u_re = jnp.zeros((8, TILE), F32)
                with_u_im = jnp.zeros((8, TILE), F32)
                for t in range(TD):
                    block = stack[UROW : RIGHT + 2, t * TILE : (t + 1) * TILE]
                    with_u_re = with_u_re + block * u_re[t : t + 1]
                    with_u_im = with_u_im + block * u_im[t : t + 1]
                with_u_re = jnp.sum(with_u_re, axis=1, keepdims=True)
                with_u_im = jnp.sum(with_u_im, axis=1, keepdims=True)
                last = UROW + 2 * it
                packed = jnp.where(lane == last, with_u_re, jnp.where(lane == last + 1, with_u_im, packed))
            wait_for(halo.at[turn], halo_send.at[turn])
            wait_for(tiles.at[pl.ds(0, ns - 1)], tile_send.at[turn])

        part = packed[0:4] + pltpu.roll(packed[4:8], 64, 1)
        for stage in range(stages):
            sums[step, stage, places[stage]] = part
            send_sum(sums, (step,), sum_send, sum_recv, stage)
            part = finish_sum(sums, (step,), sum_send, sum_recv, stage)
        reduced = jnp.concatenate([part, pltpu.roll(part, 64, 1)], axis=0)

        def entry(i, j):
            return jnp.broadcast_to(reduced[i : i + 1, j : j + 1], (8, TILE))

        def line_of(i):
            return jnp.broadcast_to(reduced[i : i + 1, :], (8, TILE))

        y_re, y_im = solve(entry)
        with_re = jnp.zeros((8, TILE), F32)
        with_im = jnp.zeros((8, TILE), F32)
        sol_re = jnp.zeros((8, TILE), F32)
        sol_im = jnp.zeros((8, TILE), F32)
        for j in range(ITERS):
            a, b = line_of(2 + 2 * j), line_of(3 + 2 * j)
            with_re = with_re + (y_re[j] * a - y_im[j] * b)
            with_im = with_im + (y_re[j] * b + y_im[j] * a)
            here, after = lane == ZROW + 2 * j, lane == ZROW + 2 * j + 1
            sol_re = jnp.where(here, y_re[j], jnp.where(after, -y_im[j], sol_re))
            sol_im = jnp.where(here, y_im[j], jnp.where(after, y_re[j], sol_im))

        def back(a, n):
            return pltpu.roll(a, TILE - n, 1)

        on_basis, on_prev = lane < NB, lane == PREV
        h_re = jnp.where(
            on_basis, with_re + back(with_im, NB), jnp.where(on_prev, with_re + back(with_im, 1), 0.0)
        )
        h_im = jnp.where(
            on_basis, with_im - back(with_re, NB), jnp.where(on_prev, with_im - back(with_re, 1), 0.0)
        )
        h_re, h_im = h_re / total_rows, h_im / total_rows
        on_imag, on_prev_imag = (lane >= NB) & (lane < 2 * NB), lane == PREV + 1
        e_re = h_re - jnp.where(
            on_imag, pltpu.roll(h_im, NB, 1), jnp.where(on_prev_imag, pltpu.roll(h_im, 1, 1), 0.0)
        )
        e_im = h_im + jnp.where(
            on_imag, pltpu.roll(h_re, NB, 1), jnp.where(on_prev_imag, pltpu.roll(h_re, 1, 1), 0.0)
        )

        @pl.when(step == 0)
        def _():
            whole = finish_sum(basis_sums, (), basis_send, basis_recv, stages - 1)
            blocks = [whole] + [pltpu.roll(whole, TILE - shift, 1) for shift in (32, 64, 96)]
            basis_gram[0:NB, :] = jnp.where(lane2 < 2 * NB, jnp.concatenate(blocks, axis=0), 0.0)

        pair = jnp.where(row == 0, e_re, jnp.where(row == 1, e_im, 0.0))
        turned = jnp.dot(pair[:, 0:NB], basis_gram[0:NB, :], precision=HIGH, preferred_element_type=F32)
        p_re = jnp.broadcast_to(h_re[0:1, PREV : PREV + 1], (8, TILE))
        p_im = jnp.broadcast_to(h_im[0:1, PREV : PREV + 1], (8, TILE))
        prev_re, prev_im = line_of(0), line_of(1)
        v_re, v_im = p_re * prev_re - p_im * prev_im, p_im * prev_re + p_re * prev_im
        share = jnp.where(lane < PREV, 2.0, jnp.where(lane < PREV + 2, 1.0, 0.0))
        first_row = (
            sol_re * with_re
            + sol_im * with_im
            - 2.0 * total_rows * (h_re * h_re + h_im * h_im)
            + share * (v_re * e_re + v_im * e_im)
        )
        first_row = jnp.where(lane < UROW, first_row, 0.0)
        each = turned * pair + jnp.where(row == 0, first_row, 0.0)
        squares = jnp.sum(jnp.sum(each, axis=0, keepdims=True), axis=1, keepdims=True)
        squares = jnp.broadcast_to(squares, (8, TILE))
        norm = jnp.sqrt(jnp.maximum(squares, 0.0) / total_rows + EPSILON)

        coef = jnp.where(row == 0, sol_re - e_re, jnp.where(row == 1, sol_im - e_im, 0.0)) / norm
        latest = jnp.dot(coef[:, 0:UROW], stack[0:UROW, :], precision=HIGH, preferred_element_type=F32)
        made[step] = latest[0:2]
        stack[PREV : PREV + 2, :] = latest[0:2]
        top = jnp.where(on_basis, h_re, jnp.where(lane == NB, back(h_re, NB), norm))
        low = jnp.where(on_basis, h_im, jnp.where(lane == NB, back(h_im, NB), 0.0))
        listed[step, 0:1, :] = top[0:1, 0 : NB + 2]
        listed[step, 1:2, :] = low[0:1, 0 : NB + 2]

    @pl.loop(0, steps)
    def _(step):
        one_step(step)


def hand_over(made, listed, made_out, listed_out):
    made_out[...] = made[...]
    listed_out[...] = listed[...]


def solution(mesh, y_chips=None):
    ns, n_dom = mesh.shape["sub"], mesh.shape["dom"]
    nz = Z_CHIPS if y_chips is None else n_dom // CORES // y_chips
    sizes = (n_dom // (CORES * nz), nz, CORES, ns)
    most = max(ns, sizes[0], nz * CORES)

    def local(basis, compact, weights, fresh, shifts, k_tiles, pattern, mass, precond, c_tiles, c_rows, c_side, c_count):
        vmem = pl.BlockSpec(memory_space=pltpu.VMEM)
        anywhere = pl.BlockSpec(memory_space=pl.ANY)
        steps = weights.shape[0]
        rows = TD * TILE
        made, listed = pl.pallas_call(
            functools.partial(kernel, sizes),
            out_shape=(
                jax.ShapeDtypeStruct((steps, 2, rows), F32),
                jax.ShapeDtypeStruct((steps, 2, NB + 2), F32),
            ),
            in_specs=[anywhere] * 3 + [pl.BlockSpec(memory_space=pltpu.SMEM)] + [anywhere] * 9,
            out_specs=(vmem, vmem),
            scratch_shapes=[
                pltpu.VMEM((TD, 3, TILE, TILE), F32),
                pltpu.VMEM((TD, 2, TILE, TILE), F32),
                pltpu.VMEM((TD, TILE, TILE), F32),
                pltpu.VMEM((rows, 6 * TILE), BF16),
                pltpu.VMEM((rows, 4 * TILE), BF16),
                pltpu.VMEM((rows, 2 * TILE), BF16),
                pltpu.VMEM((XROWS, rows), F32),
                pltpu.VMEM((TILE, TILE), F32),
                pltpu.VMEM((8, TILE), F32),
                pltpu.VMEM((steps, 8, TILE), F32),
                pltpu.VMEM((2 * NB, TILE), F32),
                pltpu.VMEM((2, 2, TD, TILE), F32),
                pltpu.VMEM((ns, 2, TD, TILE), F32),
                pltpu.VMEM((ns, 2, TD, TILE), F32),
                pltpu.VMEM((ns, 2, TD, TILE), F32),
                pltpu.VMEM((steps * ITERS, 2, 2, TD, TILE), F32),
                pltpu.VMEM((steps, 3, most, 4, TILE), F32),
                pltpu.VMEM((3, most, 4, TILE), F32),
                pltpu.VMEM((TD, 64), F32),
                pltpu.SMEM((2, TD), jnp.int32),
                pltpu.SMEM((TD,), jnp.int32),
                pltpu.SMEM((TD,), jnp.int32),
                pltpu.SMEM((steps, 2), F32),
                pltpu.VMEM(weights.shape, F32),
                pltpu.VMEM((2, NB, weights.shape[2]), F32),
                pltpu.VMEM(fresh.shape, F32),
                pltpu.VMEM((TD, TILE), F32),
                pltpu.SemaphoreType.DMA((13,)),
                pltpu.SemaphoreType.DMA((steps * ITERS,)),
                pltpu.SemaphoreType.DMA((steps * ITERS,)),
                pltpu.SemaphoreType.DMA((steps * ITERS,)),
                pltpu.SemaphoreType.DMA((steps * ITERS,)),
                pltpu.SemaphoreType.DMA((steps, 3)),
                pltpu.SemaphoreType.DMA((steps, 3)),
                pltpu.SemaphoreType.DMA((3,)),
                pltpu.SemaphoreType.DMA((3,)),
            ],
            compiler_params=pltpu.CompilerParams(collective_id=0, has_side_effects=True),
        )(
            pattern.T,
            c_rows,
            c_side,
            c_count,
            shifts,
            weights,
            jnp.swapaxes(compact, 1, 2),
            fresh,
            mass.reshape(TD, TILE),
            basis,
            k_tiles,
            precond,
            c_tiles,
        )
        return pl.pallas_call(
            hand_over,
            out_shape=(
                jax.ShapeDtypeStruct((steps, 2, rows), F32),
                jax.ShapeDtypeStruct((steps, 2, NB + 2), F32),
            ),
            in_specs=[vmem] * 2,
            out_specs=(vmem, vmem),
        )(made, listed)

    both = ("dom", "sub")
    placed = (
        P(None, None, both),
        P(),
        P(),
        P(),
        P(),
        P(both, None, None, None),
        P(both, None),
        P(both),
        P(both, None, None, None),
        P(both, None, None),
        P(both),
        P(both),
        P(both),
    )
    return jax.shard_map(
        local, mesh=mesh, in_specs=placed, out_specs=(P(None, None, both), P()), check_vma=False
    )
```
